32 devices in a mesh: space: 8 (over y, x, core), src: 4 (over z).
Axes of the slice: x: 2, y: 2, z: 4, core: 2. Of those that a mesh axis runs over, the one named last changes fastest.
Arguments:
- potential_start: float32 [16, 4, 128, 1024], P('src', None, 'space'), may hold values from -6 to 6
- adjoint_start: float32 [16, 4, 128, 1024], P('src', None, 'space'), may hold values from -6 to 6
- conductivity: float32 [4, 128, 1024], P(None, 'space', 'src'), may hold values from 0.1 to 1
- electrodes: int32 [16, 2], P('src'), may hold values from 0 to 131071
- receivers: int32 [16, 32, 2], P('src'), may hold values from 0 to 131071
- observed: float32 [16, 32], P('src'), may hold values from -6 to 6
Outputs:
- gradient: float32 [4, 128, 1024], P(None, 'space', 'src')
The draws below stay inside these ranges and needn't reach their ends.
Inputs may be any that keep to these rules, and one draw needn't show every extreme that they name: `electrodes`: each entry is a surface node id row * 1024 + column. `receivers`: each entry is a surface node id row * 1024 + column.
All inputs are finite; a program needn't handle non-finite values.
Results may differ from the reference program's by a relative error of at most 0.00002.
Values sent between devices are 32-bit elements; how exact they have to be, the bound alone decides.
No kernel may reach another device: no remote copies, remote signals or barrier semaphores. Data moves between devices by JAX's collectives and lax.ppermute only.
A program may use at most 64 MiB of HBM per device.

```python
import math
import jax
import jax.numpy as jnp
from jax import lax

NY = 1024
NZ = 4
SWEEPS = 4
RECEIVERS = 32
NX = 128
SOURCES = 16


def set_ends(values, rng, least, high):
    longest = values.shape.index(max(values.shape))
    spots = []
    for shift in (0, 1):
        where = [jax.random.randint(jax.random.fold_in(rng, axis), (), 0, length) for axis, length in enumerate(values.shape)]
        where[longest] = (where[longest] + shift) % values.shape[longest]
        spots.append(tuple(where))
    return values.at[spots[0]].set(least).at[spots[1]].set(high)


def shard_levels(own_key, dims, split, least, high):
    def one(position, shards_of):
        steps = jax.random.uniform(jax.random.fold_in(jax.random.fold_in(own_key, 6), position), (shards_of,), jnp.float32, least / len(split), high / len(split))
        return jnp.repeat(jnp.exp(steps), dims[position] // shards_of).reshape((-1,) + (1,) * (len(dims) - position - 1))

    loudness = one(*split[0])
    for cut in split[1:]:
        loudness = loudness * one(*cut)
    return loudness


def normal_values(stream_key, shape, deviation, limit, cuts=(), kind=jnp.bfloat16):
    result = jax.random.normal(stream_key, shape, jnp.float32) * deviation
    if len(cuts) > 0:
        result = shard_levels(stream_key, shape, cuts, -0.22, 0.18) * result
    return jnp.clip(result, min=-limit, max=limit).astype(kind)


def setup_inputs(seed: int = 0) -> dict:
    key_of = jax.random.split(jax.random.key(seed), 7)
    return {
        "potential_start": normal_values(key_of[0], (SOURCES, NZ, NX, NY), 1.0, 6.0, ((0, 4), (2, 8)), jnp.float32),
        "adjoint_start": normal_values(key_of[1], (SOURCES, NZ, NX, NY), 1.0, 6.0, ((0, 4), (2, 8)), jnp.float32),
        "conductivity": jnp.clip(jnp.exp(math.log(1.0) - 2.3025851 * jax.random.uniform(key_of[2], (NZ, NX, NY), jnp.float32) ** shard_levels(key_of[2], (NZ, NX, NY), ((1, 8), (2, 4)), -0.2, 0.2)), 0.1, 1.0),
        "electrodes": set_ends(jax.random.randint(key_of[3], (SOURCES, 2), 0, NX * NY), jax.random.fold_in(key_of[3], 1), 0, (NX * NY) - 1).astype(jnp.int32),
        "receivers": set_ends(jax.random.randint(key_of[4], (SOURCES, RECEIVERS, 2), 0, NX * NY), jax.random.fold_in(key_of[4], 1), 0, (NX * NY) - 1).astype(jnp.int32),
        "observed": normal_values(key_of[5], (SOURCES, RECEIVERS), 1.0, 6.0, ((0, 4),), jnp.float32),
    }


GAMMA = 0.5
CURRENT = 4.0
THETA = 1.025
DELTA = 0.975
RATIO = THETA / DELTA


def pad_axis(field, dimension, margin):
    widths = [(0, 0)] * field.ndim
    widths[dimension % field.ndim] = (margin, margin)
    return jnp.pad(field, widths)


def coefficients(padded_sigma):
    centre_sigma = padded_sigma[:, 1:-1, :]
    layer_pad = pad_axis(centre_sigma, 0, 1)
    column_pad = pad_axis(centre_sigma, 2, 1)
    face_terms = (0.5 * (centre_sigma + padded_sigma[:, :-2, :]),
                  0.5 * (centre_sigma + padded_sigma[:, 2:, :]),
                  0.5 * (centre_sigma + column_pad[:, :, :-2]),
                  0.5 * (centre_sigma + column_pad[:, :, 2:]),
                  0.5 * (centre_sigma + layer_pad[:-2]),
                  0.5 * (centre_sigma + layer_pad[2:]))
    diagonal = face_terms[0] + face_terms[1] + face_terms[2] + face_terms[3] + face_terms[4] + face_terms[5] + GAMMA * centre_sigma
    return face_terms, diagonal


def apply_operator(padded, face_terms, diagonal):
    centre = padded[..., 1:-1, :]
    layer_pad = pad_axis(centre, -3, 1)
    column_pad = pad_axis(centre, -1, 1)
    neighbours = (face_terms[0] * padded[..., :-2, :] + face_terms[1] * padded[..., 2:, :]
                  + face_terms[2] * column_pad[..., :-2] + face_terms[3] * column_pad[..., 2:]
                  + face_terms[4] * layer_pad[..., :-2, :, :] + face_terms[5] * layer_pad[..., 2:, :, :])
    return diagonal * centre - neighbours


def chebyshev(initial, source, face_terms, diagonal, inverse, extend, inside_rows):
    residual = source - apply_operator(extend(initial), face_terms, diagonal)
    if inside_rows is not None:
        residual = residual * inside_rows
    direction = inverse * residual / THETA
    factor = 1.0 / RATIO
    potential = initial
    for sweep in range(SWEEPS):
        potential = potential + direction
        if sweep + 1 < SWEEPS:
            residual = residual - apply_operator(extend(direction), face_terms, diagonal)
            if inside_rows is not None:
                residual = residual * inside_rows
            factor_next = 1.0 / (2.0 * RATIO - factor)
            direction = (factor_next * factor) * direction + (2.0 * factor_next / DELTA) * inverse * residual
            factor = factor_next
    return potential


def sensitivity(forward_pad, adjoint_pad):
    forward_mid = forward_pad[..., 1:-1, :]
    adjoint_mid = adjoint_pad[..., 1:-1, :]
    forward_layer = pad_axis(forward_mid, -3, 1)
    adjoint_layer = pad_axis(adjoint_mid, -3, 1)
    forward_column = pad_axis(forward_mid, -1, 1)
    adjoint_column = pad_axis(adjoint_mid, -1, 1)
    pairs = ((forward_pad[..., :-2, :], adjoint_pad[..., :-2, :]),
             (forward_pad[..., 2:, :], adjoint_pad[..., 2:, :]),
             (forward_column[..., :-2], adjoint_column[..., :-2]),
             (forward_column[..., 2:], adjoint_column[..., 2:]),
             (forward_layer[..., :-2, :, :], adjoint_layer[..., :-2, :, :]),
             (forward_layer[..., 2:, :, :], adjoint_layer[..., 2:, :, :]))
    running = GAMMA * forward_mid * adjoint_mid
    for forward_near, adjoint_near in pairs:
        running = running + 0.5 * (forward_mid - forward_near) * (adjoint_mid - adjoint_near)
    return -running


def local_pad(field):
    return pad_axis(field, -2, 1)


def reference_plane(node_ids, amounts):
    flat = jnp.zeros((NX * NY,), jnp.float32).at[node_ids].add(amounts)
    plane = flat.reshape(1, NX, NY)
    return jnp.concatenate([plane, jnp.zeros((NZ - 1, NX, NY), jnp.float32)], axis=0)


def reference(potential_start, adjoint_start, conductivity, electrodes, receivers, observed):
    padded_sigma = pad_axis(conductivity, 1, 1)
    face_terms, diagonal = coefficients(padded_sigma)
    inverse = 1.0 / diagonal
    currents = jnp.array([CURRENT, -CURRENT], jnp.float32)

    def per_source(running, pieces):
        initial, adjoint_init, injection, receiver_pair, measured = pieces
        forward = chebyshev(initial, reference_plane(injection, currents), face_terms, diagonal, inverse, local_pad, None)
        surface = forward[0].reshape(-1)
        predicted = surface[receiver_pair[:, 0]] - surface[receiver_pair[:, 1]]
        misfit = predicted - measured
        adjoint_source = reference_plane(jnp.concatenate([receiver_pair[:, 0], receiver_pair[:, 1]]),
                                         jnp.concatenate([misfit, -misfit]))
        adjoint = chebyshev(adjoint_init, adjoint_source, face_terms, diagonal, inverse, local_pad, None)
        return running + sensitivity(local_pad(forward), local_pad(adjoint)), None

    running, unused = lax.scan(per_source, jnp.zeros((NZ, NX, NY), jnp.float32),
                               (potential_start, adjoint_start, electrodes, receivers, observed))
    return running
```

```python
import functools

import jax
import jax.numpy as jnp
from jax import lax
from jax.experimental import pallas as pl
from jax.experimental.pallas import tpu as pltpu
from jax.sharding import PartitionSpec as P

SWEEPS = 4
GAMMA = 0.5
CURRENT = 4.0
THETA = 1.025
DELTA = 0.975
RATIO = THETA / DELTA
LANES = 128
HALO = SWEEPS + 1

VMEM = pl.BlockSpec(memory_space=pltpu.VMEM)
SMEM = pl.BlockSpec(memory_space=pltpu.SMEM)


def recurrence():
    steps = [(THETA - 1.0, 0.0, 1.0)]
    before, scale = 1.0, 1.0 / THETA
    factor = 1.0 / RATIO
    for _ in range(SWEEPS - 1):
        factor_next = 1.0 / (2.0 * RATIO - factor)
        alpha = factor_next * factor
        beta = 2.0 * factor_next / DELTA
        after = beta * scale
        steps.append(((1.0 + alpha - beta) / beta, alpha * before / after, 1.0 / scale))
        before, scale, factor = scale, after, factor_next
    return steps, scale


STEPS, FINAL = recurrence()


def rows_of(start, count, groups):
    begin = start * groups
    if not isinstance(begin, int):
        begin = pl.multiple_of(begin, groups)
    return pl.ds(begin, count * groups)


def to_rows(read, write, rows, groups):
    for j in range(groups):
        write(pl.ds(j, rows, stride=groups), read(pl.ds(j * LANES, LANES)))


def from_right(v, last_lane):
    groups = v.shape[0]
    turned = pltpu.roll(v, LANES - 1, 1)
    return jnp.where(last_lane, pltpu.roll(turned, groups - 1, 0), turned)


def from_left(v, first_lane):
    turned = pltpu.roll(v, 1, 1)
    return jnp.where(first_lane, pltpu.roll(turned, 1, 0), turned)


def lane_masks(groups):
    lane = lax.broadcasted_iota(jnp.int32, (groups, LANES), 1)
    group = lax.broadcasted_iota(jnp.int32, (groups, LANES), 0)
    first_lane = lane == 0
    last_lane = lane == LANES - 1
    first_column = first_lane & (group == 0)
    last_column = last_lane & (group == groups - 1)
    return first_lane, last_lane, first_column, last_column


def three_parts(x):
    high = x.astype(jnp.bfloat16)
    rest = x - high.astype(jnp.float32)
    middle = rest.astype(jnp.bfloat16)
    low = (rest - middle.astype(jnp.float32)).astype(jnp.bfloat16)
    return jnp.concatenate([high, middle, low], axis=0)


def column_hits(columns, j):
    nodes = columns.shape[1]
    c = lax.broadcasted_iota(jnp.int32, (LANES, nodes), 0) + j * LANES
    return jnp.where(c == columns, 1.0, 0.0).astype(jnp.bfloat16)


def halo_kernel(groups, x_ref, top_ref, bottom_ref, work):
    sources, layers, rows, _ = x_ref.shape
    for s in range(sources):
        for l in range(layers):
            for j in range(groups):
                work[s, l, pl.ds(j, rows, stride=groups), :] = x_ref[s, l, :, j * LANES : (j + 1) * LANES]
    top_ref[...] = work[:, :, : HALO * groups, :]
    bottom_ref[...] = work[:, :, (rows - HALO) * groups :, :]


def make_halos(x):
    sources, layers, rows, columns = x.shape
    groups = columns // LANES
    shape = jax.ShapeDtypeStruct((sources, layers, HALO * groups, LANES), jnp.float32)
    return pl.pallas_call(
        functools.partial(halo_kernel, groups),
        out_shape=(shape, shape),
        in_specs=[VMEM],
        out_specs=(VMEM, VMEM),
        scratch_shapes=[pltpu.VMEM((sources, layers, rows * groups, LANES), jnp.float32)],
        name="halo",
    )(x)


def sigma_kernel(groups, me_ref, *refs):
    pieces, (own_ref, top_ref, bottom_ref, stage) = refs[:-4], refs[-4:]
    count = len(pieces)
    layers, rows, share = pieces[0].shape
    me = me_ref[0]
    for k, piece in enumerate(pieces):
        stage[me ^ k] = piece[...]
    per = share // LANES
    for q in range(count):
        for l in range(layers):
            for t in range(per):
                own_ref[l, pl.ds(q * per + t, rows, stride=groups), :] = stage[
                    q, l, :, t * LANES : (t + 1) * LANES
                ]
    top_ref[...] = own_ref[:, : HALO * groups, :]
    bottom_ref[...] = own_ref[:, (rows - HALO) * groups :, :]


def assemble_sigma(me, pieces, groups):
    layers, rows, share = pieces[0].shape
    halo = jax.ShapeDtypeStruct((layers, HALO * groups, LANES), jnp.float32)
    return pl.pallas_call(
        functools.partial(sigma_kernel, groups),
        out_shape=(jax.ShapeDtypeStruct((layers, rows * groups, LANES), jnp.float32), halo, halo),
        in_specs=[SMEM] + [VMEM] * len(pieces),
        out_specs=(VMEM, VMEM, VMEM),
        scratch_shapes=[pltpu.VMEM((len(pieces), layers, rows, share), jnp.float32)],
        name="sigma",
    )(me, *pieces)


def coefficient_rows(sigma, coef, surface, groups, first, last):
    layers = sigma.shape[0]
    first_lane, last_lane, first_column, last_column = lane_masks(groups)

    def body(e, carry):
        here = rows_of(e, 1, groups)
        above = rows_of(e - 1, 1, groups)
        below = rows_of(e + 1, 1, groups)
        centre = [sigma[l, here, :] for l in range(layers)]
        for l in range(layers):
            c = centre[l]
            up = 0.5 * (c + sigma[l, above, :])
            down = 0.5 * (c + sigma[l, below, :])
            left = 0.5 * (c + jnp.where(first_column, 0.0, from_left(c, first_lane)))
            right = 0.5 * (c + jnp.where(last_column, 0.0, from_right(c, last_lane)))
            lower = 0.5 * (c + centre[l - 1]) if l > 0 else 0.5 * c
            upper = 0.5 * (c + centre[l + 1]) if l + 1 < layers else 0.5 * c
            diagonal = up + down + left + right + lower + upper + GAMMA * c
            inside = c > 0.0
            inverse = jnp.where(inside, 1.0 / jnp.where(inside, diagonal, 1.0), 0.0)
            coef[0, l, here, :] = up * inverse
            coef[1, l, here, :] = down * inverse
            coef[2, l, here, :] = jnp.where(first_column, 0.0, left * inverse)
            coef[3, l, here, :] = jnp.where(last_column, 0.0, right * inverse)
            if l > 0:
                coef[4, l, here, :] = lower * inverse
            if l + 1 < layers:
                coef[5, l, here, :] = upper * inverse
            if l == 0:
                surface[here, :] = inverse
        return carry

    lax.fori_loop(first, last, body, 0)


def sweep(step, old, new, coef, plane, groups, first, last):
    p, q, g = STEPS[step]
    sources, layers = old.shape[:2]
    first_lane, last_lane, _, _ = lane_masks(groups)

    def body(e, carry):
        here = rows_of(e, 1, groups)
        above = rows_of(e - 1, 1, groups)
        below = rows_of(e + 1, 1, groups)
        for l in range(layers):
            weight = [coef[i, l, here, :] for i in range(4)]
            lower = coef[4, l, here, :] if l > 0 else None
            upper = coef[5, l, here, :] if l + 1 < layers else None
            for s in range(sources):
                v = old[s, l, here, :]
                total = p * v
                total += weight[0] * old[s, l, above, :]
                total += weight[1] * old[s, l, below, :]
                total += weight[2] * from_left(v, first_lane)
                total += weight[3] * from_right(v, last_lane)
                if lower is not None:
                    total += lower * old[s, l - 1, here, :]
                if upper is not None:
                    total += upper * old[s, l + 1, here, :]
                if step > 0:
                    total -= q * new[s, l, here, :]
                if l == 0 and plane is not None:
                    amount = plane[s, here, :]
                    total += amount if g == 1.0 else g * amount
                new[s, l, here, :] = total
        return carry

    lax.fori_loop(first, last, body, 0)


def widen(x_ref, top_ref, bottom_ref, wide, groups):
    sources, layers, rows, _ = x_ref.shape
    for s in range(sources):
        for l in range(layers):
            for j in range(groups):
                wide[s, l, pl.ds(HALO * groups + j, rows, stride=groups), :] = x_ref[
                    s, l, :, j * LANES : (j + 1) * LANES
                ]
    wide[:, :, : HALO * groups, :] = top_ref[...]
    wide[:, :, (HALO + rows) * groups :, :] = bottom_ref[...]


def forward_kernel(
    groups, position_ref, electrodes_ref, sigma_ref, sigma_top, sigma_bottom, x_ref, top_ref, bottom_ref, nodes_ref,
    coef, surface, last_field, readings_ref, sigma, other, plane,
):
    sources, layers, rows, columns = x_ref.shape
    extent = rows + 2 * HALO
    first_row = position_ref[0] * rows
    sigma[:, : HALO * groups, :] = sigma_top[...]
    sigma[:, HALO * groups : (HALO + rows) * groups, :] = sigma_ref[...]
    sigma[:, (HALO + rows) * groups :, :] = sigma_bottom[...]
    widen(x_ref, top_ref, bottom_ref, last_field, groups)
    coefficient_rows(sigma, coef, surface, groups, 1, extent - 1)

    plane[...] = jnp.zeros(plane.shape, jnp.float32)
    column = lax.broadcasted_iota(jnp.int32, (groups, LANES), 0) * LANES + lax.broadcasted_iota(
        jnp.int32, (groups, LANES), 1
    )
    for s in range(sources):
        for k, current in enumerate((CURRENT, -CURRENT)):
            node = electrodes_ref[s, k]
            row = node // columns
            e = row - first_row + HALO
            inside = (e >= 1) & (e < extent - 1)
            here = rows_of(jnp.clip(e, 1, extent - 2), 1, groups)
            hit = (column == node - row * columns) & inside
            plane[s, here, :] += jnp.where(hit, current * surface[here, :], 0.0)

    old, new = last_field, other
    for step in range(SWEEPS):
        sweep(step, old, new, coef, plane, groups, 1 + step, extent - 1 - step)
        old, new = new, old

    node = nodes_ref[...]
    node_row = node // columns
    node_column = node - node_row * columns
    count = node.shape[1]
    picked = jnp.zeros((3 * sources * rows, count), jnp.float32)
    for j in range(groups):
        tile = jnp.concatenate(
            [old[s, 0, pl.ds(HALO * groups + j, rows, stride=groups), :] for s in range(sources)], axis=0
        )
        picked += jnp.dot(three_parts(tile), column_hits(node_column, j), preferred_element_type=jnp.float32)
    size = sources * rows
    picked = picked[:size] + picked[size : 2 * size] + picked[2 * size :]
    r = lax.broadcasted_iota(jnp.int32, (size, count), 0)
    k = lax.broadcasted_iota(jnp.int32, (size, count), 1)
    hit = (r // rows == k // (count // sources)) & (node_row - first_row == r % rows)
    readings_ref[...] = FINAL * jnp.sum(jnp.where(hit, picked, 0.0), axis=0, keepdims=True)


def forward_solve(position, electrodes, sigma, sigma_top, sigma_bottom, x, top, bottom, nodes):
    sources, layers, rows, columns = x.shape
    groups = columns // LANES
    tall = (rows + 2 * HALO) * groups
    f32 = jnp.float32
    return pl.pallas_call(
        functools.partial(forward_kernel, groups),
        out_shape=(
            jax.ShapeDtypeStruct((6, layers, tall, LANES), f32),
            jax.ShapeDtypeStruct((tall, LANES), f32),
            jax.ShapeDtypeStruct((sources, layers, tall, LANES), f32),
            jax.ShapeDtypeStruct((1, nodes.shape[1]), f32),
        ),
        in_specs=[SMEM, SMEM] + [VMEM] * 7,
        out_specs=(VMEM,) * 4,
        scratch_shapes=[
            pltpu.VMEM((layers, tall, LANES), f32),
            pltpu.VMEM((sources, layers, tall, LANES), f32),
            pltpu.VMEM((sources, tall, LANES), f32),
        ],
        name="forward",
    )(position, electrodes, sigma, sigma_top, sigma_bottom, x, top, bottom, nodes)


def adjoint_first_kernel(groups, x_ref, top_ref, bottom_ref, coef, wide, new):
    rows = x_ref.shape[2]
    widen(x_ref, top_ref, bottom_ref, wide, groups)
    sweep(0, wide, new, coef, None, groups, 1, rows + 2 * HALO - 1)


def adjoint_first(x, top, bottom, coef):
    sources, layers, rows, columns = x.shape
    groups = columns // LANES
    shape = jax.ShapeDtypeStruct((sources, layers, (rows + 2 * HALO) * groups, LANES), jnp.float32)
    return pl.pallas_call(
        functools.partial(adjoint_first_kernel, groups),
        out_shape=(shape, shape),
        in_specs=[VMEM] * 4,
        out_specs=(VMEM, VMEM),
        name="adjoint_first",
    )(x, top, bottom, coef)


def adjoint_kernel(
    rows, columns, position_ref, nodes_ref, readings_ref, observed_ref, wide_in, new_in, coef, surface, forward,
    *refs,
):
    blocks, (wide, new, plane, gradient, staged) = refs[:-5], refs[-5:]
    sources, layers, tall, _ = wide.shape
    groups = columns // LANES
    extent = tall // groups
    count = nodes_ref.shape[1]
    per_source = count // sources
    receivers = per_source // 2
    first_row = position_ref[0] * rows

    lane = lax.broadcasted_iota(jnp.int32, (1, count), 1)
    positive = (lane // receivers) % 2 == 0
    readings = readings_ref[...]
    partner = jnp.where(
        positive, pltpu.roll(readings, count - receivers, 1), pltpu.roll(readings, receivers, 1)
    )
    amounts = readings - partner - jnp.where(positive, observed_ref[...], -observed_ref[...])
    node = nodes_ref[...]
    node_row = node // columns
    node_column = node - node_row * columns
    span = extent - 2
    size = sources * span
    r = lax.broadcasted_iota(jnp.int32, (size, count), 0)
    k = lax.broadcasted_iota(jnp.int32, (size, count), 1)
    hit = (r // span == k // per_source) & (node_row - first_row + HALO - 1 == r % span)
    spread = three_parts(jnp.where(hit, amounts, 0.0))
    for j in range(groups):
        part = lax.dot_general(
            spread, column_hits(node_column, j), (((1,), (1,)), ((), ())), preferred_element_type=jnp.float32
        )
        part = part[:size] + part[size : 2 * size] + part[2 * size :]
        weight = surface[pl.ds(groups + j, span, stride=groups), :]
        for s in range(sources):
            plane[s, pl.ds(groups + j, span, stride=groups), :] = part[s * span : (s + 1) * span] * weight

    def copy_in(e, carry):
        here = rows_of(e, 1, groups)
        for s in range(sources):
            for l in range(layers):
                wide[s, l, here, :] = wide_in[s, l, here, :]
                fresh = new_in[s, l, here, :]
                new[s, l, here, :] = fresh + plane[s, here, :] if l == 0 else fresh
        return carry

    lax.fori_loop(1, extent - 1, copy_in, 0)

    old, newer = new, wide
    for step in range(1, SWEEPS):
        sweep(step, old, newer, coef, plane, groups, 1 + step, extent - 1 - step)
        old, newer = newer, old
    adjoint = old

    first_lane, last_lane, first_column, last_column = lane_masks(groups)

    def pair(s, l, e):
        here = rows_of(e, 1, groups)
        return forward[s, l, here, :], adjoint[s, l, here, :]

    def body(e, above_faces):
        below_faces = []
        products, layer_faces, right_faces = [], [], []
        for l in range(layers):
            product = row_face = right_face = layer_face = None
            for s in range(sources):
                u, a = pair(s, l, e)
                u_below, a_below = pair(s, l, e + 1)
                u_right = jnp.where(last_column, 0.0, from_right(u, last_lane))
                a_right = jnp.where(last_column, 0.0, from_right(a, last_lane))
                terms = [u * a, (u - u_below) * (a - a_below), (u - u_right) * (a - a_right)]
                if l + 1 < layers:
                    u_next, a_next = pair(s, l + 1, e)
                    terms.append((u - u_next) * (a - a_next))
                if s == 0:
                    sums = terms
                else:
                    sums = [x + y for x, y in zip(sums, terms)]
            products.append(sums[0])
            below_faces.append(sums[1])
            right_faces.append(sums[2])
            layer_faces.append(sums[3] if l + 1 < layers else sums[0])
        for l in range(layers):
            left_face = jnp.where(first_column, products[l], from_left(right_faces[l], first_lane))
            total = products[l] + above_faces[l] + below_faces[l] + right_faces[l] + left_face
            total += layer_faces[l] + (layer_faces[l - 1] if l > 0 else products[l])
            gradient[l, rows_of(e - HALO, 1, groups), :] = (-0.5 * FINAL * FINAL) * total
        return tuple(below_faces)

    start = []
    for l in range(layers):
        running = None
        for s in range(sources):
            u, a = pair(s, l, HALO - 1)
            u_below, a_below = pair(s, l, HALO)
            term = (u - u_below) * (a - a_below)
            running = term if s == 0 else running + term
        start.append(running)
    lax.fori_loop(HALO, HALO + rows, body, tuple(start))

    me = position_ref[1]
    count_blocks = len(blocks)
    per = groups // count_blocks
    for q in range(count_blocks):
        for l in range(layers):
            for t in range(per):
                staged[q, l, :, t * LANES : (t + 1) * LANES] = gradient[
                    l, pl.ds(q * per + t, rows, stride=groups), :
                ]
    for i, block in enumerate(blocks):
        block[...] = staged[me ^ i]


def adjoint_solve(position, nodes, readings, observed, wide, new, coef, surface, forward, rows, columns, blocks):
    sources, layers, tall, _ = wide.shape
    groups = columns // LANES
    f32 = jnp.float32
    block = jax.ShapeDtypeStruct((layers, rows, columns // blocks), f32)
    return pl.pallas_call(
        functools.partial(adjoint_kernel, rows, columns),
        out_shape=(block,) * blocks,
        in_specs=[SMEM] + [VMEM] * 8,
        out_specs=(VMEM,) * blocks,
        scratch_shapes=[
            pltpu.VMEM((sources, layers, tall, LANES), f32),
            pltpu.VMEM((sources, layers, tall, LANES), f32),
            pltpu.VMEM((sources, tall, LANES), f32),
            pltpu.VMEM((layers, rows * groups, LANES), f32),
            pltpu.VMEM((blocks, layers, rows, columns // blocks), f32),
        ],
        name="adjoint",
    )(position, nodes, readings, observed, wide, new, coef, surface, forward)


def is_power_of_two(n):
    return n & (n - 1) == 0


def exchange(value, axis, mask):
    count = lax.axis_size(axis)
    return lax.ppermute(value, axis, [(i, i ^ mask) for i in range(count)])


def shift_down(value, axis):
    count = lax.axis_size(axis)
    return lax.ppermute(value, axis, [(i, i + 1) for i in range(count - 1)])


def shift_up(value, axis):
    count = lax.axis_size(axis)
    return lax.ppermute(value, axis, [(i + 1, i) for i in range(count - 1)])


def sum_over(value, axis):
    count = lax.axis_size(axis)
    if not is_power_of_two(count):
        return lax.psum(value, axis)
    mask = 1
    while mask < count:
        value = value + exchange(value, axis, mask)
        mask *= 2
    return value


def per_device(potential_start, adjoint_start, conductivity, electrodes, receivers, observed):
    sources, layers, rows, columns = potential_start.shape
    groups = columns // LANES
    split = lax.axis_size("src")
    direct = is_power_of_two(split) and split <= 4 and (columns // split) % LANES == 0
    position = jnp.stack([lax.axis_index("space"), lax.axis_index("src")]).astype(jnp.int32)

    if direct:
        pieces = [conductivity] + [None] * (split - 1)
        for k in reversed(range(1, split)):
            pieces[k] = exchange(conductivity, "src", k)
        me = position[1:]
    else:
        pieces = [lax.all_gather(conductivity, "src", axis=2, tiled=True)]
        me = jnp.zeros((1,), jnp.int32)
    sigma, sigma_first, sigma_last = assemble_sigma(me, pieces, groups)
    x_first, x_last = make_halos(potential_start)
    a_first, a_last = make_halos(adjoint_start)
    x_top, x_bottom = shift_down(x_last, "space"), shift_up(x_first, "space")
    sigma_top, sigma_bottom = shift_down(sigma_last, "space"), shift_up(sigma_first, "space")
    a_top, a_bottom = shift_down(a_last, "space"), shift_up(a_first, "space")

    nodes = receivers.transpose(0, 2, 1).reshape(1, -1)
    measured = jnp.broadcast_to(observed[:, None, :], (sources, 2, observed.shape[1])).reshape(1, -1)
    coef, surface, forward, readings = forward_solve(
        position, electrodes, sigma, sigma_top, sigma_bottom, potential_start, x_top, x_bottom, nodes
    )
    readings = sum_over(readings, "space")
    wide, new = adjoint_first(adjoint_start, a_top, a_bottom, coef)
    blocks = adjoint_solve(
        position, nodes, readings, measured, wide, new, coef, surface, forward, rows, columns, split if direct else 1
    )
    if direct:
        total = blocks[0]
        for k in reversed(range(1, split)):
            total = total + exchange(blocks[k], "src", k)
        return total
    summed = lax.psum(blocks[0], "src")
    share = columns // split
    return lax.dynamic_slice_in_dim(summed, lax.axis_index("src") * share, share, 2)


def solution(mesh):
    return jax.shard_map(
        per_device,
        mesh=mesh,
        in_specs=(
            P("src", None, "space", None),
            P("src", None, "space", None),
            P(None, "space", "src"),
            P("src", None),
            P("src", None, None),
            P("src", None),
        ),
        out_specs=P(None, "space", "src"),
        check_vma=False,
    )
```

```python
import functools
import math

import jax
import jax.numpy as jnp
from jax import lax
from jax.experimental import pallas as pl
from jax.experimental.pallas import tpu as pltpu
from jax.sharding import PartitionSpec as P


SWEEPS = 4
GAMMA = 0.5
CURRENT = 4.0
THETA = 1.025
DELTA = 0.975
LANES = 128
HALO = SWEEPS + 1

VMEM = pl.BlockSpec(memory_space=pltpu.VMEM)
SMEM = pl.BlockSpec(memory_space=pltpu.SMEM)
GRANT = pltpu.CompilerParams(vmem_limit_bytes=20 * 1024 * 1024)


def product_form():
    roots = [THETA + DELTA * math.cos((2 * i + 1) * math.pi / (2 * SWEEPS)) for i in range(SWEEPS)]
    order = sorted(roots)
    order = [order[i // 2] if i % 2 == 0 else order[-1 - i // 2] for i in range(SWEEPS)]
    steps, scale = [], 1.0
    for root in order:
        steps.append((root - 1.0, 1.0 / scale))
        scale /= root
    return steps, scale


STEPS, FINAL = product_form()


def rows_of(start, count, groups):
    begin = start * groups
    if not isinstance(begin, int):
        begin = pl.multiple_of(begin, groups)
    return pl.ds(begin, count * groups)


def from_right(v, last_lane):
    groups = v.shape[0]
    turned = pltpu.roll(v, LANES - 1, 1)
    return jnp.where(last_lane, pltpu.roll(turned, groups - 1, 0), turned)


def from_left(v, first_lane):
    turned = pltpu.roll(v, 1, 1)
    return jnp.where(first_lane, pltpu.roll(turned, 1, 0), turned)


def lane_masks(groups):
    lane = lax.broadcasted_iota(jnp.int32, (groups, LANES), 1)
    group = lax.broadcasted_iota(jnp.int32, (groups, LANES), 0)
    first_lane = lane == 0
    last_lane = lane == LANES - 1
    first_column = first_lane & (group == 0)
    last_column = last_lane & (group == groups - 1)
    return first_lane, last_lane, first_column, last_column


def three_parts(x):
    high = x.astype(jnp.bfloat16)
    rest = x - high.astype(jnp.float32)
    middle = rest.astype(jnp.bfloat16)
    low = (rest - middle.astype(jnp.float32)).astype(jnp.bfloat16)
    return jnp.concatenate([high, middle, low], axis=0)


def column_hits(columns, j):
    nodes = columns.shape[1]
    c = lax.broadcasted_iota(jnp.int32, (LANES, nodes), 0) + j * LANES
    return jnp.where(c == columns, 1.0, 0.0).astype(jnp.bfloat16)


def spread_kernel(groups, x_ref, a_ref, x_wide, a_wide, first_ref, last_ref):
    sources, layers, rows, _ = x_ref.shape
    for i, (field, wide) in enumerate(((x_ref, x_wide), (a_ref, a_wide))):
        for s in range(sources):
            for l in range(layers):
                for j in range(groups):
                    wide[s, l, pl.ds(HALO * groups + j, rows, stride=groups), :] = field[
                        s, l, :, j * LANES : (j + 1) * LANES
                    ]
        first_ref[i] = wide[:, :, HALO * groups : 2 * HALO * groups, :]
        last_ref[i] = wide[:, :, rows * groups : (HALO + rows) * groups, :]


def spread_rows(x, a):
    sources, layers, rows, columns = x.shape
    groups = columns // LANES
    wide = jax.ShapeDtypeStruct((sources, layers, (rows + 2 * HALO) * groups, LANES), jnp.float32)
    halo = jax.ShapeDtypeStruct((2, sources, layers, HALO * groups, LANES), jnp.float32)
    return pl.pallas_call(
        functools.partial(spread_kernel, groups),
        out_shape=(wide, wide, halo, halo),
        in_specs=[VMEM, VMEM],
        out_specs=(VMEM,) * 4,
        compiler_params=GRANT,
        name="spread",
    )(x, a)


def nodes_kernel(receivers_ref, observed_ref, nodes_ref, measured_ref):
    sources, ends, count = receivers_ref.shape
    for s in range(sources):
        for end in range(ends):
            lanes = pl.ds((s * ends + end) * count, count)
            nodes_ref[:, lanes] = receivers_ref[s, end : end + 1, :]
            seen = observed_ref[s : s + 1, :]
            measured_ref[:, lanes] = seen if end == 0 else -seen


def lay_out_nodes(receivers, observed):
    sources, ends, count = receivers.shape
    total = sources * ends * count
    return pl.pallas_call(
        nodes_kernel,
        out_shape=(jax.ShapeDtypeStruct((1, total), jnp.int32), jax.ShapeDtypeStruct((1, total), jnp.float32)),
        in_specs=[VMEM, VMEM],
        out_specs=(VMEM, VMEM),
        compiler_params=GRANT,
        name="nodes",
    )(receivers, observed)


def sigma_kernel(groups, *refs):
    pieces, (wide_ref, first_ref, last_ref, stage) = refs[:-4], refs[-4:]
    count = len(pieces)
    layers, rows, share = pieces[0].shape
    me = lax.axis_index("src") if count > 1 else 0
    for k, piece in enumerate(pieces):
        stage[me ^ k] = piece[...]
    per = share // LANES
    for q in range(count):
        for l in range(layers):
            for t in range(per):
                wide_ref[l, pl.ds(HALO * groups + q * per + t, rows, stride=groups), :] = stage[
                    q, l, :, t * LANES : (t + 1) * LANES
                ]
    first_ref[...] = wide_ref[:, HALO * groups : 2 * HALO * groups, :]
    last_ref[...] = wide_ref[:, rows * groups : (HALO + rows) * groups, :]


def assemble_sigma(pieces, groups):
    layers, rows, share = pieces[0].shape
    wide = jax.ShapeDtypeStruct((layers, (rows + 2 * HALO) * groups, LANES), jnp.float32)
    halo = jax.ShapeDtypeStruct((layers, HALO * groups, LANES), jnp.float32)
    return pl.pallas_call(
        functools.partial(sigma_kernel, groups),
        out_shape=(wide, halo, halo),
        in_specs=[VMEM] * len(pieces),
        out_specs=(VMEM, VMEM, VMEM),
        scratch_shapes=[pltpu.VMEM((len(pieces), layers, rows, share), jnp.float32)],
        compiler_params=GRANT,
        name="sigma",
    )(*pieces)


def row_numbers(segments):
    (first, middle), count = segments[0], segments[0][1] - segments[0][0]
    if len(segments) == 1:
        return count, lambda i: first + i
    start, end = segments[1]

    def number(i):
        if isinstance(i, int):
            return first + i if i < count else start + i - count
        return first + i + jnp.where(i >= count, start - middle, 0)

    return count + end - start, number


def coefficient_rows(sigma, coef, surface, groups, segments):
    layers = sigma.shape[0]
    first_lane, last_lane, first_column, last_column = lane_masks(groups)
    count, number = row_numbers(segments)

    def body(i, carry):
        e = number(i)
        here = rows_of(e, 1, groups)
        above = rows_of(e - 1, 1, groups)
        below = rows_of(e + 1, 1, groups)
        centre = [sigma[l, here, :] for l in range(layers)]
        for l in range(layers):
            c = centre[l]
            up = 0.5 * (c + sigma[l, above, :])
            down = 0.5 * (c + sigma[l, below, :])
            left = 0.5 * (c + jnp.where(first_column, 0.0, from_left(c, first_lane)))
            right = 0.5 * (c + jnp.where(last_column, 0.0, from_right(c, last_lane)))
            lower = 0.5 * (c + centre[l - 1]) if l > 0 else 0.5 * c
            upper = 0.5 * (c + centre[l + 1]) if l + 1 < layers else 0.5 * c
            diagonal = up + down + left + right + lower + upper + GAMMA * c
            inside = c > 0.0
            inverse = jnp.where(inside, 1.0 / jnp.where(inside, diagonal, 1.0), 0.0)
            coef[0, l, here, :] = up * inverse
            coef[1, l, here, :] = down * inverse
            coef[2, l, here, :] = jnp.where(first_column, 0.0, left * inverse)
            coef[3, l, here, :] = jnp.where(last_column, 0.0, right * inverse)
            if l > 0:
                coef[4, l, here, :] = lower * inverse
            if l + 1 < layers:
                coef[5, l, here, :] = upper * inverse
            if l == 0:
                surface[here, :] = inverse
        return carry

    lax.fori_loop(0, count, body, 0)


def sweep(step, old, new, coef, plane, shifted, groups, segments):
    p, g = STEPS[step]
    sources, layers = old.shape[:2]
    first_lane, last_lane, _, _ = lane_masks(groups)
    count, number = row_numbers(segments)

    def turn(e):
        here = rows_of(e, 1, groups)
        before = pl.ds(e * groups - 1, groups)
        after = pl.ds(e * groups + 1, groups)
        for l in range(layers):
            for s in range(sources):
                v = old[s, l, here, :]
                shifted[0, s, l] = pltpu.roll(jnp.where(last_lane, old[s, l, before, :], v), 1, 1)
                shifted[1, s, l] = pltpu.roll(jnp.where(first_lane, old[s, l, after, :], v), LANES - 1, 1)

    def row(e):
        here = rows_of(e, 1, groups)
        above = rows_of(e - 1, 1, groups)
        below = rows_of(e + 1, 1, groups)
        for l in range(layers):
            weight = [coef[i, l, here, :] for i in range(4)]
            lower = coef[4, l, here, :] if l > 0 else None
            upper = coef[5, l, here, :] if l + 1 < layers else None
            for s in range(sources):
                total = p * old[s, l, here, :]
                total += weight[0] * old[s, l, above, :]
                total += weight[1] * old[s, l, below, :]
                total += weight[2] * shifted[0, s, l]
                total += weight[3] * shifted[1, s, l]
                if lower is not None:
                    total += lower * old[s, l - 1, here, :]
                if upper is not None:
                    total += upper * old[s, l + 1, here, :]
                if l == 0 and plane is not None:
                    amount = plane[s, here, :]
                    total += amount if g == 1.0 else g * amount
                new[s, l, here, :] = total

    def body(i, carry):
        row(number(i))
        turn(number(i + 1))
        return carry

    turn(number(0))
    lax.fori_loop(0, count - 1, body, 0)
    row(number(count - 1))


def inner_rows(step, rows):
    return [(HALO + 1 + step, HALO + rows - 1 - step)]


def outer_rows(step, rows):
    return [(1 + step, HALO + 1 + step), (HALO + rows - 1 - step, 2 * HALO + rows - 1 - step)]


def add_electrodes(electrodes_ref, plane, surface, rows, groups, segments):
    columns = groups * LANES
    first_row = lax.axis_index("space") * rows
    lowest, highest = segments[0][0], segments[-1][1] - 1
    column = lax.broadcasted_iota(jnp.int32, (groups, LANES), 0) * LANES + lax.broadcasted_iota(
        jnp.int32, (groups, LANES), 1
    )
    for s in range(plane.shape[0]):
        for k, current in enumerate((CURRENT, -CURRENT)):
            node = electrodes_ref[k, s]
            row = node // columns
            e = row - first_row + HALO
            inside = functools.reduce(jnp.logical_or, [(e >= a) & (e < b) for a, b in segments])
            here = rows_of(jnp.clip(e, lowest, highest), 1, groups)
            hit = (column == node - row * columns) & inside
            plane[s, here, :] += jnp.where(hit, current * surface[here, :], 0.0)


def inner_kernel(groups, electrodes_ref, sigma, _, wide, coef, surface, other, plane, shifted):
    rows = wide.shape[2] // groups - 2 * HALO
    segments = inner_rows(0, rows)
    coefficient_rows(sigma, coef, surface, groups, segments)
    plane[...] = jnp.zeros(plane.shape, jnp.float32)
    add_electrodes(electrodes_ref, plane, surface, rows, groups, segments)
    old, new = wide, other
    for step in range(SWEEPS):
        sweep(step, old, new, coef, plane, shifted, groups, inner_rows(step, rows))
        old, new = new, old


def inner_solve(groups, electrodes, sigma, wide):
    sources, layers, tall, _ = wide.shape
    f32 = jnp.float32
    return pl.pallas_call(
        functools.partial(inner_kernel, groups),
        out_shape=(
            jax.ShapeDtypeStruct(wide.shape, f32),
            jax.ShapeDtypeStruct((6, layers, tall, LANES), f32),
            jax.ShapeDtypeStruct((tall, LANES), f32),
            jax.ShapeDtypeStruct(wide.shape, f32),
            jax.ShapeDtypeStruct((sources, tall, LANES), f32),
        ),
        in_specs=[SMEM, VMEM, VMEM],
        out_specs=(VMEM,) * 5,
        scratch_shapes=[pltpu.VMEM((2, sources, layers, groups, LANES), f32)],
        input_output_aliases={2: 0},
        compiler_params=GRANT,
        name="inner",
    )(electrodes, sigma, wide)


def outer_kernel(
    groups, electrodes_ref, sigma_top, sigma_bottom, top_ref, bottom_ref, nodes_ref, *refs
):
    sigma, wide, coef, surface, other, plane, readings_ref, shifted = refs[6:]
    sources, _, tall, _ = wide.shape
    columns = groups * LANES
    rows = tall // groups - 2 * HALO
    first_row = lax.axis_index("space") * rows
    bottom = (HALO + rows) * groups
    sigma[:, : HALO * groups, :] = sigma_top[...]
    sigma[:, bottom:, :] = sigma_bottom[...]
    wide[:, :, : HALO * groups, :] = top_ref[0]
    wide[:, :, bottom:, :] = bottom_ref[0]
    segments = outer_rows(0, rows)
    coefficient_rows(sigma, coef, surface, groups, segments)
    add_electrodes(electrodes_ref, plane, surface, rows, groups, segments)
    old, new = wide, other
    for step in range(SWEEPS):
        sweep(step, old, new, coef, plane, shifted, groups, outer_rows(step, rows))
        old, new = new, old

    node = nodes_ref[...]
    node_row = node // columns
    node_column = node - node_row * columns
    count = node.shape[1]
    picked = jnp.zeros((3 * sources * rows, count), jnp.float32)
    for j in range(groups):
        tile = jnp.concatenate(
            [old[s, 0, pl.ds(HALO * groups + j, rows, stride=groups), :] for s in range(sources)], axis=0
        )
        picked += jnp.dot(three_parts(tile), column_hits(node_column, j), preferred_element_type=jnp.float32)
    size = sources * rows
    picked = picked[:size] + picked[size : 2 * size] + picked[2 * size :]
    r = lax.broadcasted_iota(jnp.int32, (size, count), 0)
    k = lax.broadcasted_iota(jnp.int32, (size, count), 1)
    hit = (r // rows == k // (count // sources)) & (node_row - first_row == r % rows)
    readings_ref[...] = FINAL * jnp.sum(jnp.where(hit, picked, 0.0), axis=0, keepdims=True)


def outer_solve(groups, electrodes, sigma_top, sigma_bottom, top, bottom, nodes, sigma, inner):
    carried = (sigma,) + tuple(inner)
    sources, layers = inner[0].shape[:2]
    f32 = jnp.float32
    kept = tuple(jax.ShapeDtypeStruct(x.shape, f32) for x in carried)
    return pl.pallas_call(
        functools.partial(outer_kernel, groups),
        out_shape=kept + (jax.ShapeDtypeStruct((1, nodes.shape[1]), f32),),
        in_specs=[SMEM] + [VMEM] * 11,
        out_specs=(VMEM,) * 7,
        scratch_shapes=[pltpu.VMEM((2, sources, layers, groups, LANES), f32)],
        input_output_aliases={6 + i: i for i in range(6)},
        compiler_params=GRANT,
        name="outer",
    )(electrodes, sigma_top, sigma_bottom, top, bottom, nodes, *carried)


def begin_kernel(groups, start, end, top_ref, bottom_ref, coef, *refs):
    wide, new, shifted = refs[-3:]
    if start == 1:
        rows = wide.shape[2] // groups - 2 * HALO
        wide[:, :, : HALO * groups, :] = top_ref[1]
        wide[:, :, (HALO + rows) * groups :, :] = bottom_ref[1]
    sweep(0, wide, new, coef, None, shifted, groups, [(start, end)])


def begin_adjoint(groups, part, top, bottom, coef, wide, new):
    f32 = jnp.float32
    shape = jax.ShapeDtypeStruct(wide.shape, f32)
    arguments = (top, bottom, coef, wide) + (() if new is None else (new,))
    return pl.pallas_call(
        functools.partial(begin_kernel, groups, part[0], part[-1] + 1),
        out_shape=(shape, shape),
        in_specs=[VMEM] * len(arguments),
        out_specs=(VMEM, VMEM),
        scratch_shapes=[pltpu.VMEM((2,) + wide.shape[:2] + (groups, LANES), f32)],
        input_output_aliases={3: 0} if new is None else {3: 0, 4: 1},
        compiler_params=GRANT,
        name="begin",
    )(*arguments)


def adjoint_kernel(groups, parts, nodes_ref, observed_ref, coef, surface, forward, *refs):
    readings_refs, refs = refs[:parts], refs[parts + 2 :]
    (wide, new), blocks, (plane, gradient, staged, shifted) = refs[:2], refs[2:-4], refs[-4:]
    sources, layers, tall, _ = wide.shape
    columns = groups * LANES
    extent = tall // groups
    rows = extent - 2 * HALO
    count = nodes_ref.shape[1]
    per_source = count // sources
    receivers = per_source // 2
    first_row = lax.axis_index("space") * rows

    lane = lax.broadcasted_iota(jnp.int32, (1, count), 1)
    positive = (lane // receivers) % 2 == 0
    readings = sum(part[...] for part in readings_refs)
    partner = jnp.where(
        positive, pltpu.roll(readings, count - receivers, 1), pltpu.roll(readings, receivers, 1)
    )
    amounts = readings - partner - observed_ref[...]
    node = nodes_ref[...]
    node_row = node // columns
    node_column = node - node_row * columns
    span = extent - 2
    size = sources * span
    r = lax.broadcasted_iota(jnp.int32, (size, count), 0)
    k = lax.broadcasted_iota(jnp.int32, (size, count), 1)
    hit = (r // span == k // per_source) & (node_row - first_row + HALO - 1 == r % span)
    spread = three_parts(jnp.where(hit, amounts, 0.0))
    for j in range(groups):
        part = lax.dot_general(
            spread, column_hits(node_column, j), (((1,), (1,)), ((), ())), preferred_element_type=jnp.float32
        )
        part = part[:size] + part[size : 2 * size] + part[2 * size :]
        where = pl.ds(groups + j, span, stride=groups)
        weight = surface[where, :]
        for s in range(sources):
            amount = part[s * span : (s + 1) * span] * weight
            plane[s, where, :] = amount
            new[s, 0, where, :] += amount

    old, newer = new, wide
    for step in range(1, SWEEPS):
        sweep(step, old, newer, coef, plane, shifted, groups, [(1 + step, extent - 1 - step)])
        old, newer = newer, old
    adjoint = old

    first_lane, _, first_column, last_column = lane_masks(groups)
    both = (forward, adjoint)

    def turn(e):
        here = rows_of(e, 1, groups)
        after = pl.ds(e * groups + 1, groups)
        for i, field in enumerate(both):
            for l in range(layers):
                for s in range(sources):
                    v = jnp.where(first_lane, field[s, l, after, :], field[s, l, here, :])
                    shifted[i, s, l] = pltpu.roll(v, LANES - 1, 1)

    def row(e, above_faces):
        here = rows_of(e, 1, groups)
        below = rows_of(e + 1, 1, groups)
        sums = []
        for l in range(layers):
            for s in range(sources):
                u, a = forward[s, l, here, :], adjoint[s, l, here, :]
                terms = [
                    u * a,
                    (u - forward[s, l, below, :]) * (a - adjoint[s, l, below, :]),
                    (u - shifted[0, s, l]) * (a - shifted[1, s, l]),
                ]
                if l + 1 < layers:
                    terms.append((u - forward[s, l + 1, here, :]) * (a - adjoint[s, l + 1, here, :]))
                total = terms if s == 0 else [x + y for x, y in zip(total, terms)]
            sums.append(total)
        for l in range(layers):
            product, down, right = sums[l][:3]
            right = jnp.where(last_column, product, right)
            left = jnp.where(first_column, product, from_left(right, first_lane))
            upper = sums[l][3] if l + 1 < layers else product
            lower = sums[l - 1][3] if l > 0 else product
            total = product + above_faces[l] + down + right + left + lower + upper
            gradient[l, rows_of(e - HALO, 1, groups), :] = (-0.5 * FINAL * FINAL) * total
        return tuple(sums[l][1] for l in range(layers))

    above_faces = []
    for l in range(layers):
        for s in range(sources):
            above, here = rows_of(HALO - 1, 1, groups), rows_of(HALO, 1, groups)
            term = (forward[s, l, above, :] - forward[s, l, here, :]) * (
                adjoint[s, l, above, :] - adjoint[s, l, here, :]
            )
            total = term if s == 0 else total + term
        above_faces.append(total)

    def body(e, above_faces):
        above_faces = row(e, above_faces)
        turn(e + 1)
        return above_faces

    turn(HALO)
    above_faces = lax.fori_loop(HALO, HALO + rows - 1, body, tuple(above_faces))
    row(HALO + rows - 1, above_faces)

    count_blocks = len(blocks)
    me = lax.axis_index("src") if count_blocks > 1 else 0
    per = groups // count_blocks
    for q in range(count_blocks):
        for l in range(layers):
            for t in range(per):
                staged[q, l, :, t * LANES : (t + 1) * LANES] = gradient[
                    l, pl.ds(q * per + t, rows, stride=groups), :
                ]
    for i, block in enumerate(blocks):
        block[...] = staged[me ^ i]


def finish_adjoint(groups, nodes, readings, observed, wide, new, coef, surface, forward, blocks):
    sources, layers, tall, _ = wide.shape
    rows = tall // groups - 2 * HALO
    columns = groups * LANES
    f32 = jnp.float32
    block = jax.ShapeDtypeStruct((layers, rows, columns // blocks), f32)
    shape = jax.ShapeDtypeStruct(wide.shape, f32)
    parts = len(readings)
    return pl.pallas_call(
        functools.partial(adjoint_kernel, groups, parts),
        out_shape=(shape, shape) + (block,) * blocks,
        in_specs=[VMEM] * (7 + parts),
        out_specs=(VMEM,) * (2 + blocks),
        scratch_shapes=[
            pltpu.VMEM((sources, tall, LANES), f32),
            pltpu.VMEM((layers, rows * groups, LANES), f32),
            pltpu.VMEM((blocks, layers, rows, columns // blocks), f32),
            pltpu.VMEM((2, sources, layers, groups, LANES), f32),
        ],
        input_output_aliases={5 + parts: 0, 6 + parts: 1},
        compiler_params=GRANT,
        name="adjoint",
    )(nodes, observed, coef, surface, forward, *readings, wide, new)[2:]


def is_power_of_two(n):
    return n & (n - 1) == 0


def exchange(value, axis, mask):
    count = lax.axis_size(axis)
    return lax.ppermute(value, axis, [(i, i ^ mask) for i in range(count)])


def shift_down(value, axis):
    count = lax.axis_size(axis)
    return lax.ppermute(value, axis, [(i, i + 1) for i in range(count - 1)])


def shift_up(value, axis):
    count = lax.axis_size(axis)
    return lax.ppermute(value, axis, [(i + 1, i) for i in range(count - 1)])


def shares(first, last, parts):
    cuts = [first + (last - first) * i // parts for i in range(parts + 1)]
    return [range(a, b) for a, b in zip(cuts, cuts[1:])]


def per_device(potential_start, adjoint_start, conductivity, electrodes, receivers, observed):
    _, _, rows, columns = potential_start.shape
    groups = columns // LANES
    split, strips = lax.axis_size("src"), lax.axis_size("space")
    direct = is_power_of_two(split) and split <= 4 and (columns // split) % LANES == 0

    if direct:
        pieces = [conductivity] + [None] * (split - 1)
        for k in reversed(range(1, split)):
            pieces[k] = exchange(conductivity, "src", k)
    else:
        pieces = [lax.all_gather(conductivity, "src", axis=2, tiled=True)]
    x_wide, a_wide, first, last = spread_rows(potential_start, adjoint_start)
    top = shift_down(last, "space")
    bottom = shift_up(first, "space")
    nodes, measured = lay_out_nodes(receivers.transpose(0, 2, 1), observed)
    sigma, sigma_first, sigma_last = assemble_sigma(pieces, groups)
    sigma_top = shift_down(sigma_last, "space")
    sigma_bottom = shift_up(sigma_first, "space")
    ends = electrodes.T
    inner = inner_solve(groups, ends, sigma, x_wide)
    _, forward, coef, surface, _, _, readings = outer_solve(
        groups, ends, sigma_top, sigma_bottom, top, bottom, nodes, sigma, inner
    )

    begun = None
    if is_power_of_two(strips):
        rounds = strips.bit_length() - 1
        parts = shares(1, rows + 2 * HALO - 1, max(rounds, 1))
        for i in range(rounds):
            other = exchange(readings, "space", 1 << i)
            a_wide, begun = begin_adjoint(groups, parts[i], top, bottom, coef, a_wide, begun)
            if i + 1 < rounds:
                readings = readings + other
        terms = [readings, other] if rounds else [readings]
        parts = parts[rounds:]
    else:
        terms = [lax.psum(readings, "space")]
        parts = shares(1, rows + 2 * HALO - 1, 1)
    for part in parts:
        a_wide, begun = begin_adjoint(groups, part, top, bottom, coef, a_wide, begun)
    blocks = finish_adjoint(
        groups, nodes, terms, measured, a_wide, begun, coef, surface, forward, split if direct else 1
    )
    if direct:
        total = blocks[0]
        for k in reversed(range(1, split)):
            total = total + exchange(blocks[k], "src", k)
        return total
    summed = lax.psum(blocks[0], "src")
    share = columns // split
    return lax.dynamic_slice_in_dim(summed, lax.axis_index("src") * share, share, 2)


def solution(mesh):
    return jax.shard_map(
        per_device,
        mesh=mesh,
        in_specs=(
            P("src", None, "space", None),
            P("src", None, "space", None),
            P(None, "space", "src"),
            P("src", None),
            P("src", None, None),
            P("src", None),
        ),
        out_specs=P(None, "space", "src"),
        check_vma=False,
    )
```

```python
import functools
import math

import jax
import jax.numpy as jnp
from jax import lax
from jax.experimental import pallas as pl
from jax.experimental.pallas import tpu as pltpu
from jax.sharding import PartitionSpec as P


SWEEPS = 4
GAMMA = 0.5
CURRENT = 4.0
THETA = 1.025
DELTA = 0.975
LANES = 128
HALO = SWEEPS + 1

VMEM = pl.BlockSpec(memory_space=pltpu.VMEM)
SMEM = pl.BlockSpec(memory_space=pltpu.SMEM)
GRANT = pltpu.CompilerParams(vmem_limit_bytes=20 * 1024 * 1024)


def product_form():
    roots = [THETA + DELTA * math.cos((2 * i + 1) * math.pi / (2 * SWEEPS)) for i in range(SWEEPS)]
    order = sorted(roots)
    order = [order[i // 2] if i % 2 == 0 else order[-1 - i // 2] for i in range(SWEEPS)]
    steps, scale = [], 1.0
    for root in order:
        steps.append((root - 1.0, 1.0 / scale))
        scale /= root
    return steps, scale


STEPS, FINAL = product_form()


def rows_of(start, count, groups):
    begin = start * groups
    if not isinstance(begin, int):
        begin = pl.multiple_of(begin, groups)
    return pl.ds(begin, count * groups)


def from_right(v, last_lane):
    groups = v.shape[0]
    turned = pltpu.roll(v, LANES - 1, 1)
    return jnp.where(last_lane, pltpu.roll(turned, groups - 1, 0), turned)


def from_left(v, first_lane):
    turned = pltpu.roll(v, 1, 1)
    return jnp.where(first_lane, pltpu.roll(turned, 1, 0), turned)


def lane_masks(groups):
    lane = lax.broadcasted_iota(jnp.int32, (groups, LANES), 1)
    group = lax.broadcasted_iota(jnp.int32, (groups, LANES), 0)
    first_lane = lane == 0
    last_lane = lane == LANES - 1
    first_column = first_lane & (group == 0)
    last_column = last_lane & (group == groups - 1)
    return first_lane, last_lane, first_column, last_column


def three_parts(x):
    high = x.astype(jnp.bfloat16)
    rest = x - high.astype(jnp.float32)
    middle = rest.astype(jnp.bfloat16)
    low = (rest - middle.astype(jnp.float32)).astype(jnp.bfloat16)
    return jnp.concatenate([high, middle, low], axis=0)


def column_hits(columns, j):
    nodes = columns.shape[1]
    c = lax.broadcasted_iota(jnp.int32, (LANES, nodes), 0) + j * LANES
    return jnp.where(c == columns, 1.0, 0.0).astype(jnp.bfloat16)


def facing(axis, rows, groups, sent):
    even = lax.rem(lax.axis_index(axis), 2) == 0
    low, high = (HALO, rows) if sent else (0, HALO + rows)
    return [
        pl.ds(pl.multiple_of(jnp.where(condition, high, low) * groups, groups), HALO * groups)
        for condition in (even, jnp.logical_not(even))
    ]


def spread_kernel(groups, x_ref, wide, inner_ref, outer_ref):
    sources, layers, rows, _ = x_ref.shape
    for s in range(sources):
        for l in range(layers):
            for j in range(groups):
                wide[s, l, pl.ds(HALO * groups + j, rows, stride=groups), :] = x_ref[
                    s, l, :, j * LANES : (j + 1) * LANES
                ]
    to_inner, to_outer = facing("space", rows, groups, True)
    inner_ref[...] = wide[:, :, to_inner, :]
    outer_ref[...] = wide[:, :, to_outer, :]


def spread_rows(x):
    sources, layers, rows, columns = x.shape
    groups = columns // LANES
    wide = jax.ShapeDtypeStruct((sources, layers, (rows + 2 * HALO) * groups, LANES), jnp.float32)
    halo = jax.ShapeDtypeStruct((sources, layers, HALO * groups, LANES), jnp.float32)
    return pl.pallas_call(
        functools.partial(spread_kernel, groups),
        out_shape=(wide, halo, halo),
        in_specs=[VMEM],
        out_specs=(VMEM,) * 3,
        compiler_params=GRANT,
        name="spread",
    )(x)


def nodes_kernel(receivers_ref, observed_ref, nodes_ref, measured_ref):
    sources, ends, count = receivers_ref.shape
    for s in range(sources):
        for end in range(ends):
            lanes = pl.ds((s * ends + end) * count, count)
            nodes_ref[:, lanes] = receivers_ref[s, end : end + 1, :]
            seen = observed_ref[s : s + 1, :]
            measured_ref[:, lanes] = seen if end == 0 else -seen


def lay_out_nodes(receivers, observed):
    sources, ends, count = receivers.shape
    total = sources * ends * count
    return pl.pallas_call(
        nodes_kernel,
        out_shape=(jax.ShapeDtypeStruct((1, total), jnp.int32), jax.ShapeDtypeStruct((1, total), jnp.float32)),
        in_specs=[VMEM, VMEM],
        out_specs=(VMEM, VMEM),
        compiler_params=GRANT,
        name="nodes",
    )(receivers, observed)


def sigma_kernel(groups, *refs):
    pieces, (wide_ref, inner_ref, outer_ref, stage) = refs[:-4], refs[-4:]
    count = len(pieces)
    layers, rows, share = pieces[0].shape
    me = lax.axis_index("src") if count > 1 else 0
    for k, piece in enumerate(pieces):
        stage[me ^ k] = piece[...]
    per = share // LANES
    for q in range(count):
        for l in range(layers):
            for t in range(per):
                wide_ref[l, pl.ds(HALO * groups + q * per + t, rows, stride=groups), :] = stage[
                    q, l, :, t * LANES : (t + 1) * LANES
                ]
    to_inner, to_outer = facing("space", rows, groups, True)
    inner_ref[...] = wide_ref[:, to_inner, :]
    outer_ref[...] = wide_ref[:, to_outer, :]


def assemble_sigma(pieces, groups):
    layers, rows, share = pieces[0].shape
    wide = jax.ShapeDtypeStruct((layers, (rows + 2 * HALO) * groups, LANES), jnp.float32)
    halo = jax.ShapeDtypeStruct((layers, HALO * groups, LANES), jnp.float32)
    return pl.pallas_call(
        functools.partial(sigma_kernel, groups),
        out_shape=(wide, halo, halo),
        in_specs=[VMEM] * len(pieces),
        out_specs=(VMEM, VMEM, VMEM),
        scratch_shapes=[pltpu.VMEM((len(pieces), layers, rows, share), jnp.float32)],
        compiler_params=GRANT,
        name="sigma",
    )(*pieces)


def row_numbers(segments):
    (first, middle), count = segments[0], segments[0][1] - segments[0][0]
    if len(segments) == 1:
        return count, lambda i: first + i
    start, end = segments[1]

    def number(i):
        if isinstance(i, int):
            return first + i if i < count else start + i - count
        return first + i + jnp.where(i >= count, start - middle, 0)

    return count + end - start, number


def coefficient_rows(sigma, coef, surface, groups, segments):
    layers = sigma.shape[0]
    first_lane, last_lane, first_column, last_column = lane_masks(groups)
    count, number = row_numbers(segments)

    def body(i, carry):
        e = number(i)
        here = rows_of(e, 1, groups)
        above = rows_of(e - 1, 1, groups)
        below = rows_of(e + 1, 1, groups)
        centre = [sigma[l, here, :] for l in range(layers)]
        for l in range(layers):
            c = centre[l]
            up = 0.5 * (c + sigma[l, above, :])
            down = 0.5 * (c + sigma[l, below, :])
            left = 0.5 * (c + jnp.where(first_column, 0.0, from_left(c, first_lane)))
            right = 0.5 * (c + jnp.where(last_column, 0.0, from_right(c, last_lane)))
            lower = 0.5 * (c + centre[l - 1]) if l > 0 else 0.5 * c
            upper = 0.5 * (c + centre[l + 1]) if l + 1 < layers else 0.5 * c
            diagonal = up + down + left + right + lower + upper + GAMMA * c
            inside = c > 0.0
            inverse = jnp.where(inside, 1.0 / jnp.where(inside, diagonal, 1.0), 0.0)
            coef[0, l, here, :] = up * inverse
            coef[1, l, here, :] = down * inverse
            coef[2, l, here, :] = jnp.where(first_column, 0.0, left * inverse)
            coef[3, l, here, :] = jnp.where(last_column, 0.0, right * inverse)
            if l > 0:
                coef[4, l, here, :] = lower * inverse
            if l + 1 < layers:
                coef[5, l, here, :] = upper * inverse
            if l == 0:
                surface[here, :] = inverse
        return carry

    lax.fori_loop(0, count, body, 0)


def sweep(step, old, new, coef, plane, shifted, groups, segments):
    p, g = STEPS[step]
    sources, layers = old.shape[:2]
    first_lane, last_lane, _, _ = lane_masks(groups)
    count, number = row_numbers(segments)

    def turn(e):
        here = rows_of(e, 1, groups)
        before = pl.ds(e * groups - 1, groups)
        after = pl.ds(e * groups + 1, groups)
        for l in range(layers):
            for s in range(sources):
                v = old[s, l, here, :]
                shifted[0, s, l] = pltpu.roll(jnp.where(last_lane, old[s, l, before, :], v), 1, 1)
                shifted[1, s, l] = pltpu.roll(jnp.where(first_lane, old[s, l, after, :], v), LANES - 1, 1)

    def row(e):
        here = rows_of(e, 1, groups)
        above = rows_of(e - 1, 1, groups)
        below = rows_of(e + 1, 1, groups)
        for l in range(layers):
            weight = [coef[i, l, here, :] for i in range(4)]
            lower = coef[4, l, here, :] if l > 0 else None
            upper = coef[5, l, here, :] if l + 1 < layers else None
            for s in range(sources):
                total = p * old[s, l, here, :]
                total += weight[0] * old[s, l, above, :]
                total += weight[1] * old[s, l, below, :]
                total += weight[2] * shifted[0, s, l]
                total += weight[3] * shifted[1, s, l]
                if lower is not None:
                    total += lower * old[s, l - 1, here, :]
                if upper is not None:
                    total += upper * old[s, l + 1, here, :]
                if l == 0 and plane is not None:
                    amount = plane[s, here, :]
                    total += amount if g == 1.0 else g * amount
                new[s, l, here, :] = total

    def body(i, carry):
        row(number(i))
        turn(number(i + 1))
        return carry

    turn(number(0))
    lax.fori_loop(0, count - 1, body, 0)
    row(number(count - 1))


def inner_rows(step, rows):
    return [(HALO + 1 + step, HALO + rows - 1 - step)]


def outer_rows(step, rows):
    return [(1 + step, HALO + 1 + step), (HALO + rows - 1 - step, 2 * HALO + rows - 1 - step)]


def add_electrodes(electrodes_ref, plane, surface, rows, groups, segments):
    columns = groups * LANES
    first_row = lax.axis_index("space") * rows
    lowest, highest = segments[0][0], segments[-1][1] - 1
    column = lax.broadcasted_iota(jnp.int32, (groups, LANES), 0) * LANES + lax.broadcasted_iota(
        jnp.int32, (groups, LANES), 1
    )
    for s in range(plane.shape[0]):
        for k, current in enumerate((CURRENT, -CURRENT)):
            node = electrodes_ref[k, s]
            row = node // columns
            e = row - first_row + HALO
            inside = functools.reduce(jnp.logical_or, [(e >= a) & (e < b) for a, b in segments])
            here = rows_of(jnp.clip(e, lowest, highest), 1, groups)
            hit = (column == node - row * columns) & inside
            plane[s, here, :] += jnp.where(hit, current * surface[here, :], 0.0)


def inner_kernel(groups, electrodes_ref, sigma, _, wide, coef, surface, other, plane, shifted):
    rows = wide.shape[2] // groups - 2 * HALO
    segments = inner_rows(0, rows)
    coefficient_rows(sigma, coef, surface, groups, segments)
    plane[...] = jnp.zeros(plane.shape, jnp.float32)
    add_electrodes(electrodes_ref, plane, surface, rows, groups, segments)
    old, new = wide, other
    for step in range(SWEEPS):
        sweep(step, old, new, coef, plane, shifted, groups, inner_rows(step, rows))
        old, new = new, old


def inner_solve(groups, electrodes, sigma, wide):
    sources, layers, tall, _ = wide.shape
    f32 = jnp.float32
    return pl.pallas_call(
        functools.partial(inner_kernel, groups),
        out_shape=(
            jax.ShapeDtypeStruct(wide.shape, f32),
            jax.ShapeDtypeStruct((6, layers, tall, LANES), f32),
            jax.ShapeDtypeStruct((tall, LANES), f32),
            jax.ShapeDtypeStruct(wide.shape, f32),
            jax.ShapeDtypeStruct((sources, tall, LANES), f32),
        ),
        in_specs=[SMEM, VMEM, VMEM],
        out_specs=(VMEM,) * 5,
        scratch_shapes=[pltpu.VMEM((2, sources, layers, groups, LANES), f32)],
        input_output_aliases={2: 0},
        compiler_params=GRANT,
        name="inner",
    )(electrodes, sigma, wide)


def outer_kernel(
    groups, electrodes_ref, sigma_inner, sigma_outer, inner_ref, outer_ref, nodes_ref, *refs
):
    sigma, wide, coef, surface, other, plane, readings_ref, shifted = refs[6:]
    sources, _, tall, _ = wide.shape
    columns = groups * LANES
    rows = tall // groups - 2 * HALO
    first_row = lax.axis_index("space") * rows
    from_inner, from_outer = facing("space", rows, groups, False)
    sigma[:, from_inner, :] = sigma_inner[...]
    sigma[:, from_outer, :] = sigma_outer[...]
    wide[:, :, from_inner, :] = inner_ref[...]
    wide[:, :, from_outer, :] = outer_ref[...]
    segments = outer_rows(0, rows)
    coefficient_rows(sigma, coef, surface, groups, segments)
    add_electrodes(electrodes_ref, plane, surface, rows, groups, segments)
    old, new = wide, other
    for step in range(SWEEPS):
        sweep(step, old, new, coef, plane, shifted, groups, outer_rows(step, rows))
        old, new = new, old

    node = nodes_ref[...]
    node_row = node // columns
    node_column = node - node_row * columns
    count = node.shape[1]
    picked = jnp.zeros((3 * sources * rows, count), jnp.float32)
    for j in range(groups):
        tile = jnp.concatenate(
            [old[s, 0, pl.ds(HALO * groups + j, rows, stride=groups), :] for s in range(sources)], axis=0
        )
        picked += jnp.dot(three_parts(tile), column_hits(node_column, j), preferred_element_type=jnp.float32)
    size = sources * rows
    picked = picked[:size] + picked[size : 2 * size] + picked[2 * size :]
    r = lax.broadcasted_iota(jnp.int32, (size, count), 0)
    k = lax.broadcasted_iota(jnp.int32, (size, count), 1)
    hit = (r // rows == k // (count // sources)) & (node_row - first_row == r % rows)
    readings_ref[...] = FINAL * jnp.sum(jnp.where(hit, picked, 0.0), axis=0, keepdims=True)


def outer_solve(groups, electrodes, sigma_inner, sigma_outer, from_inner, from_outer, nodes, sigma, inner):
    carried = (sigma,) + tuple(inner)
    sources, layers = inner[0].shape[:2]
    f32 = jnp.float32
    kept = tuple(jax.ShapeDtypeStruct(x.shape, f32) for x in carried)
    return pl.pallas_call(
        functools.partial(outer_kernel, groups),
        out_shape=kept + (jax.ShapeDtypeStruct((1, nodes.shape[1]), f32),),
        in_specs=[SMEM] + [VMEM] * 11,
        out_specs=(VMEM,) * 7,
        scratch_shapes=[pltpu.VMEM((2, sources, layers, groups, LANES), f32)],
        input_output_aliases={6 + i: i for i in range(6)},
        compiler_params=GRANT,
        name="outer",
    )(electrodes, sigma_inner, sigma_outer, from_inner, from_outer, nodes, *carried)


def begin_kernel(groups, segments, coef, *refs):
    wide, new, shifted = refs[-3:]
    if segments[0][0] == 1:
        rows = wide.shape[2] // groups - 2 * HALO
        from_inner, from_outer = facing("space", rows, groups, False)
        wide[:, :, from_inner, :] = refs[0][...]
        wide[:, :, from_outer, :] = refs[1][...]
    sweep(0, wide, new, coef, None, shifted, groups, segments)


def begin_adjoint(groups, segments, coef, halos, wide, new):
    f32 = jnp.float32
    shape = jax.ShapeDtypeStruct(wide.shape, f32)
    halos = halos if segments[0][0] == 1 else ()
    arguments = (coef,) + halos + (wide,) + (() if new is None else (new,))
    at = 1 + len(halos)
    return pl.pallas_call(
        functools.partial(begin_kernel, groups, segments),
        out_shape=(shape, shape),
        in_specs=[VMEM] * len(arguments),
        out_specs=(VMEM, VMEM),
        scratch_shapes=[pltpu.VMEM((2,) + wide.shape[:2] + (groups, LANES), f32)],
        input_output_aliases={at: 0} if new is None else {at: 0, at + 1: 1},
        compiler_params=GRANT,
        name="begin",
    )(*arguments)


def adjoint_kernel(groups, parts, nodes_ref, observed_ref, coef, surface, forward, *refs):
    readings_refs, refs = refs[:parts], refs[parts + 2 :]
    (wide, new), blocks, (plane, gradient, staged, shifted) = refs[:2], refs[2:-4], refs[-4:]
    sources, layers, tall, _ = wide.shape
    columns = groups * LANES
    extent = tall // groups
    rows = extent - 2 * HALO
    count = nodes_ref.shape[1]
    per_source = count // sources
    receivers = per_source // 2
    first_row = lax.axis_index("space") * rows

    lane = lax.broadcasted_iota(jnp.int32, (1, count), 1)
    positive = (lane // receivers) % 2 == 0
    readings = sum(part[...] for part in readings_refs)
    partner = jnp.where(
        positive, pltpu.roll(readings, count - receivers, 1), pltpu.roll(readings, receivers, 1)
    )
    amounts = readings - partner - observed_ref[...]
    node = nodes_ref[...]
    node_row = node // columns
    node_column = node - node_row * columns
    span = extent - 2
    size = sources * span
    r = lax.broadcasted_iota(jnp.int32, (size, count), 0)
    k = lax.broadcasted_iota(jnp.int32, (size, count), 1)
    hit = (r // span == k // per_source) & (node_row - first_row + HALO - 1 == r % span)
    spread = three_parts(jnp.where(hit, amounts, 0.0))
    for j in range(groups):
        part = lax.dot_general(
            spread, column_hits(node_column, j), (((1,), (1,)), ((), ())), preferred_element_type=jnp.float32
        )
        part = part[:size] + part[size : 2 * size] + part[2 * size :]
        where = pl.ds(groups + j, span, stride=groups)
        weight = surface[where, :]
        for s in range(sources):
            amount = part[s * span : (s + 1) * span] * weight
            plane[s, where, :] = amount
            new[s, 0, where, :] += amount

    old, newer = new, wide
    for step in range(1, SWEEPS):
        sweep(step, old, newer, coef, plane, shifted, groups, [(1 + step, extent - 1 - step)])
        old, newer = newer, old
    adjoint = old

    first_lane, _, first_column, last_column = lane_masks(groups)
    both = (forward, adjoint)

    def turn(e):
        here = rows_of(e, 1, groups)
        after = pl.ds(e * groups + 1, groups)
        for i, field in enumerate(both):
            for l in range(layers):
                for s in range(sources):
                    v = jnp.where(first_lane, field[s, l, after, :], field[s, l, here, :])
                    shifted[i, s, l] = pltpu.roll(v, LANES - 1, 1)

    def row(e, above_faces):
        here = rows_of(e, 1, groups)
        below = rows_of(e + 1, 1, groups)
        sums = []
        for l in range(layers):
            for s in range(sources):
                u, a = forward[s, l, here, :], adjoint[s, l, here, :]
                terms = [
                    u * a,
                    (u - forward[s, l, below, :]) * (a - adjoint[s, l, below, :]),
                    (u - shifted[0, s, l]) * (a - shifted[1, s, l]),
                ]
                if l + 1 < layers:
                    terms.append((u - forward[s, l + 1, here, :]) * (a - adjoint[s, l + 1, here, :]))
                total = terms if s == 0 else [x + y for x, y in zip(total, terms)]
            sums.append(total)
        for l in range(layers):
            product, down, right = sums[l][:3]
            right = jnp.where(last_column, product, right)
            left = jnp.where(first_column, product, from_left(right, first_lane))
            upper = sums[l][3] if l + 1 < layers else product
            lower = sums[l - 1][3] if l > 0 else product
            total = product + above_faces[l] + down + right + left + lower + upper
            gradient[l, rows_of(e - HALO, 1, groups), :] = (-0.5 * FINAL * FINAL) * total
        return tuple(sums[l][1] for l in range(layers))

    above_faces = []
    for l in range(layers):
        for s in range(sources):
            above, here = rows_of(HALO - 1, 1, groups), rows_of(HALO, 1, groups)
            term = (forward[s, l, above, :] - forward[s, l, here, :]) * (
                adjoint[s, l, above, :] - adjoint[s, l, here, :]
            )
            total = term if s == 0 else total + term
        above_faces.append(total)

    def body(e, above_faces):
        above_faces = row(e, above_faces)
        turn(e + 1)
        return above_faces

    turn(HALO)
    above_faces = lax.fori_loop(HALO, HALO + rows - 1, body, tuple(above_faces))
    row(HALO + rows - 1, above_faces)

    count_blocks = len(blocks)
    me = lax.axis_index("src") if count_blocks > 1 else 0
    per = groups // count_blocks
    for q in range(count_blocks):
        for l in range(layers):
            for t in range(per):
                staged[q, l, :, t * LANES : (t + 1) * LANES] = gradient[
                    l, pl.ds(q * per + t, rows, stride=groups), :
                ]
    for i, block in enumerate(blocks):
        block[...] = staged[me ^ i]


def finish_adjoint(groups, nodes, readings, observed, wide, new, coef, surface, forward, blocks):
    sources, layers, tall, _ = wide.shape
    rows = tall // groups - 2 * HALO
    columns = groups * LANES
    f32 = jnp.float32
    block = jax.ShapeDtypeStruct((layers, rows, columns // blocks), f32)
    shape = jax.ShapeDtypeStruct(wide.shape, f32)
    parts = len(readings)
    return pl.pallas_call(
        functools.partial(adjoint_kernel, groups, parts),
        out_shape=(shape, shape) + (block,) * blocks,
        in_specs=[VMEM] * (7 + parts),
        out_specs=(VMEM,) * (2 + blocks),
        scratch_shapes=[
            pltpu.VMEM((sources, tall, LANES), f32),
            pltpu.VMEM((layers, rows * groups, LANES), f32),
            pltpu.VMEM((blocks, layers, rows, columns // blocks), f32),
            pltpu.VMEM((2, sources, layers, groups, LANES), f32),
        ],
        input_output_aliases={5 + parts: 0, 6 + parts: 1},
        compiler_params=GRANT,
        name="adjoint",
    )(nodes, observed, coef, surface, forward, *readings, wide, new)[2:]


def is_power_of_two(n):
    return n & (n - 1) == 0


def exchange(value, axis, mask):
    count = lax.axis_size(axis)
    return lax.ppermute(value, axis, [(i, i ^ mask) for i in range(count)])


def neighbour_pairs(value, axis, first):
    lower = range(first, lax.axis_size(axis) - 1, 2)
    return lax.ppermute(value, axis, [(i, i + 1) for i in lower] + [(i + 1, i) for i in lower])


def per_device(potential_start, adjoint_start, conductivity, electrodes, receivers, observed):
    _, _, rows, columns = potential_start.shape
    groups = columns // LANES
    split, strips = lax.axis_size("src"), lax.axis_size("space")
    direct = is_power_of_two(split) and split <= 4 and (columns // split) % LANES == 0

    if direct:
        pieces = [conductivity] + [None] * (split - 1)
        for k in reversed(range(1, split)):
            pieces[k] = exchange(conductivity, "src", k)
    else:
        pieces = [lax.all_gather(conductivity, "src", axis=2, tiled=True)]
    x_wide, to_inner, to_outer = spread_rows(potential_start)
    from_inner = neighbour_pairs(to_inner, "space", 0)
    from_outer = neighbour_pairs(to_outer, "space", 1)
    a_wide, a_inner, a_outer = spread_rows(adjoint_start)
    a_inner = neighbour_pairs(a_inner, "space", 0)
    a_outer = neighbour_pairs(a_outer, "space", 1)
    nodes, measured = lay_out_nodes(receivers.transpose(0, 2, 1), observed)
    sigma, sigma_inner, sigma_outer = assemble_sigma(pieces, groups)
    sigma_outer = neighbour_pairs(sigma_outer, "space", 1)
    sigma_inner = neighbour_pairs(sigma_inner, "space", 0)
    ends = electrodes.T
    inner = inner_solve(groups, ends, sigma, x_wide)
    _, forward, coef, surface, _, _, readings = outer_solve(
        groups, ends, sigma_inner, sigma_outer, from_inner, from_outer, nodes, sigma, inner
    )

    parts, begun = [inner_rows(0, rows), outer_rows(0, rows)], None

    def begin(wide, new):
        return begin_adjoint(groups, parts.pop(0), coef, (a_inner, a_outer), wide, new)

    if is_power_of_two(strips):
        rounds = strips.bit_length() - 1
        for i in range(rounds):
            other = exchange(readings, "space", 1 << i)
            if i >= rounds - 2:
                a_wide, begun = begin(a_wide, begun)
            if i + 1 < rounds:
                readings = readings + other
        terms = [readings, other] if rounds else [readings]
    else:
        terms = [lax.psum(readings, "space")]
    while parts:
        a_wide, begun = begin(a_wide, begun)
    blocks = finish_adjoint(
        groups, nodes, terms, measured, a_wide, begun, coef, surface, forward, split if direct else 1
    )
    if direct:
        total = blocks[0]
        for k in reversed(range(1, split)):
            total = total + exchange(blocks[k], "src", k)
        return total
    summed = lax.psum(blocks[0], "src")
    share = columns // split
    return lax.dynamic_slice_in_dim(summed, lax.axis_index("src") * share, share, 2)


def solution(mesh):
    return jax.shard_map(
        per_device,
        mesh=mesh,
        in_specs=(
            P("src", None, "space", None),
            P("src", None, "space", None),
            P(None, "space", "src"),
            P("src", None),
            P("src", None, None),
            P("src", None),
        ),
        out_specs=P(None, "space", "src"),
        check_vma=False,
    )
```

```python
import functools
import math

import jax
import jax.numpy as jnp
from jax import lax
from jax.experimental import pallas as pl
from jax.experimental.pallas import tpu as pltpu
from jax.sharding import PartitionSpec as P


SWEEPS = 4
GAMMA = 0.5
CURRENT = 4.0
THETA = 1.025
DELTA = 0.975
LANES = 128
HALO = SWEEPS + 1
BATCH = 8

VMEM = pl.BlockSpec(memory_space=pltpu.VMEM)
SMEM = pl.BlockSpec(memory_space=pltpu.SMEM)
GRANT = pltpu.CompilerParams(vmem_limit_bytes=20 * 1024 * 1024)


def product_form():
    roots = [THETA + DELTA * math.cos((2 * i + 1) * math.pi / (2 * SWEEPS)) for i in range(SWEEPS)]
    order = sorted(roots)
    order = [order[i // 2] if i % 2 == 0 else order[-1 - i // 2] for i in range(SWEEPS)]
    steps, scale = [], 1.0
    for root in order:
        steps.append((root - 1.0, 1.0 / scale))
        scale /= root
    return steps, scale


STEPS, FINAL = product_form()


def dense(e, groups):
    begin = e * groups
    return pl.ds(begin if isinstance(begin, int) else pl.multiple_of(begin, groups), groups)


def tile(e, groups):
    begin = (2 * e + 1) * groups
    return pl.ds(begin if isinstance(begin, int) else pl.multiple_of(begin, groups), groups)


def left_of(e, groups):
    return pl.ds((2 * e + 1) * groups - 1, groups)


def right_of(e, groups):
    return pl.ds((2 * e + 1) * groups + 1, groups)


def sublane(first, j, count, groups):
    return pl.ds((2 * first + 1) * groups + j, count, stride=2 * groups)


def extent_of(wide, groups):
    return wide.shape[-2] // (2 * groups) - 1


def wide_length(rows, columns):
    return (rows + 2 * HALO + 1) * 2 * (columns // LANES)


def refill(planes, groups, first, last):
    extent = extent_of(planes[0], groups)
    for start in range(first, last, BATCH):
        start = min(start, extent - BATCH)
        for plane in planes:
            plane[sublane(start, -1, BATCH, groups), :] = pltpu.roll(
                plane[sublane(start, groups - 1, BATCH, groups), :], 1, 1
            )
            plane[sublane(start, groups, BATCH, groups), :] = pltpu.roll(
                plane[sublane(start, 0, BATCH, groups), :], LANES - 1, 1
            )


def planes_of(field, layers=None):
    layers = range(field.shape[1]) if layers is None else layers
    return [field.at[s, l] for s in range(field.shape[0]) for l in layers]


def doubled(rows):
    count = rows.shape[0]
    if count == LANES:
        return rows
    return jnp.concatenate([rows] * (LANES // count) + ([rows[: LANES % count]] if LANES % count else []), axis=0)


def columns_to_sublanes(read, write, work, groups):
    for j in range(groups):
        work[j * LANES : (j + 1) * LANES, :] = doubled(read(j)).T
    for s in range(groups):
        write(s, work[pl.ds(s, LANES, stride=groups), :].T)


def columns_to_lanes(read, write, work, groups):
    for s in range(groups):
        work[pl.ds(s, LANES, stride=groups), :] = doubled(read(s)).T
    for j in range(groups):
        write(j, work[j * LANES : (j + 1) * LANES, :].T)


def end_masks(groups):
    lane = lax.broadcasted_iota(jnp.int32, (groups, LANES), 1)
    group = lax.broadcasted_iota(jnp.int32, (groups, LANES), 0)
    return (lane == 0) & (group == 0), (lane == LANES - 1) & (group == groups - 1)


def three_parts(x):
    high = x.astype(jnp.bfloat16)
    rest = x - high.astype(jnp.float32)
    middle = rest.astype(jnp.bfloat16)
    low = (rest - middle.astype(jnp.float32)).astype(jnp.bfloat16)
    return jnp.concatenate([high, middle, low], axis=0)


def column_hits(columns, j, groups):
    nodes = columns.shape[1]
    c = lax.broadcasted_iota(jnp.int32, (LANES, nodes), 0) * groups + j
    return jnp.where(c == columns, 1.0, 0.0).astype(jnp.bfloat16)


def facing(axis, rows, sent):
    even = lax.rem(lax.axis_index(axis), 2) == 0
    low, high = (HALO, rows) if sent else (0, HALO + rows)
    return jnp.where(even, high, low), jnp.where(even, low, high)


def take_rows(wide, first, out, groups):
    for h in range(HALO):
        out[..., h * groups : (h + 1) * groups, :] = wide[..., tile(first + h, groups), :]


def put_rows(wide, first, received, groups):
    for h in range(HALO):
        wide[..., tile(first + h, groups), :] = received[..., h * groups : (h + 1) * groups, :]


def spread_kernel(groups, x_ref, wide, inner_ref, outer_ref, work):
    sources, layers, rows, _ = x_ref.shape
    fields = [(s, l) for s in range(sources) for l in range(layers)]
    per = LANES // rows
    for at in range(0, len(fields), per):
        block = fields[at : at + per]

        def read(j):
            return jnp.concatenate([x_ref[s, l, :, j * LANES : (j + 1) * LANES] for s, l in block], axis=0)

        def write(j, turned):
            for i, (s, l) in enumerate(block):
                wide[s, l, sublane(HALO, j, rows, groups), :] = turned[i * rows : (i + 1) * rows]

        columns_to_sublanes(read, write, work, groups)
    refill(planes_of(wide), groups, HALO, HALO + rows)
    to_inner, to_outer = facing("space", rows, True)
    take_rows(wide, to_inner, inner_ref, groups)
    take_rows(wide, to_outer, outer_ref, groups)


def spread_rows(x):
    sources, layers, rows, columns = x.shape
    groups = columns // LANES
    wide = jax.ShapeDtypeStruct((sources, layers, wide_length(rows, columns), LANES), jnp.float32)
    halo = jax.ShapeDtypeStruct((sources, layers, HALO * groups, LANES), jnp.float32)
    return pl.pallas_call(
        functools.partial(spread_kernel, groups),
        out_shape=(wide, halo, halo),
        in_specs=[VMEM],
        out_specs=(VMEM,) * 3,
        scratch_shapes=[pltpu.VMEM((columns, LANES), jnp.float32)],
        compiler_params=GRANT,
        name="spread",
    )(x)


def nodes_kernel(receivers_ref, observed_ref, nodes_ref, measured_ref):
    sources, ends, count = receivers_ref.shape
    for s in range(sources):
        for end in range(ends):
            lanes = pl.ds((s * ends + end) * count, count)
            nodes_ref[:, lanes] = receivers_ref[s, end : end + 1, :]
            seen = observed_ref[s : s + 1, :]
            measured_ref[:, lanes] = seen if end == 0 else -seen


def lay_out_nodes(receivers, observed):
    sources, ends, count = receivers.shape
    total = sources * ends * count
    return pl.pallas_call(
        nodes_kernel,
        out_shape=(jax.ShapeDtypeStruct((1, total), jnp.int32), jax.ShapeDtypeStruct((1, total), jnp.float32)),
        in_specs=[VMEM, VMEM],
        out_specs=(VMEM, VMEM),
        compiler_params=GRANT,
        name="nodes",
    )(receivers, observed)


def sigma_kernel(groups, *refs):
    pieces, (wide_ref, inner_ref, outer_ref, stage, work) = refs[:-5], refs[-5:]
    count = len(pieces)
    layers, rows, share = pieces[0].shape
    me = lax.axis_index("src") if count > 1 else 0
    for k, piece in enumerate(pieces):
        stage[me ^ k] = piece[...]
    per = share // LANES

    def read(j):
        return stage[j // per, :, :, (j % per) * LANES : (j % per + 1) * LANES].reshape(layers * rows, LANES)

    def write(j, turned):
        for l in range(layers):
            wide_ref[l, sublane(HALO, j, rows, groups), :] = turned[l * rows : (l + 1) * rows]

    columns_to_sublanes(read, write, work, groups)
    refill([wide_ref.at[l] for l in range(layers)], groups, HALO, HALO + rows)
    to_inner, to_outer = facing("space", rows, True)
    take_rows(wide_ref, to_inner, inner_ref, groups)
    take_rows(wide_ref, to_outer, outer_ref, groups)


def assemble_sigma(pieces, groups):
    layers, rows, share = pieces[0].shape
    columns = groups * LANES
    wide = jax.ShapeDtypeStruct((layers, wide_length(rows, columns), LANES), jnp.float32)
    halo = jax.ShapeDtypeStruct((layers, HALO * groups, LANES), jnp.float32)
    return pl.pallas_call(
        functools.partial(sigma_kernel, groups),
        out_shape=(wide, halo, halo),
        in_specs=[VMEM] * len(pieces),
        out_specs=(VMEM, VMEM, VMEM),
        scratch_shapes=[
            pltpu.VMEM((len(pieces), layers, rows, share), jnp.float32),
            pltpu.VMEM((columns, LANES), jnp.float32),
        ],
        compiler_params=GRANT,
        name="sigma",
    )(*pieces)


def row_numbers(segments):
    (first, middle), count = segments[0], segments[0][1] - segments[0][0]
    if len(segments) == 1:
        return count, lambda i: first + i
    start, end = segments[1]

    def number(i):
        if isinstance(i, int):
            return first + i if i < count else start + i - count
        return first + i + jnp.where(i >= count, start - middle, 0)

    return count + end - start, number


def coefficient_rows(sigma, coef, surface, groups, segments):
    layers = sigma.shape[0]
    first_column, last_column = end_masks(groups)
    count, number = row_numbers(segments)

    def body(i, carry):
        e = number(i)
        here = dense(e, groups)
        centre = [sigma[l, tile(e, groups), :] for l in range(layers)]
        for l in range(layers):
            c = centre[l]
            up = 0.5 * (c + sigma[l, tile(e - 1, groups), :])
            down = 0.5 * (c + sigma[l, tile(e + 1, groups), :])
            left = 0.5 * (c + jnp.where(first_column, 0.0, sigma[l, left_of(e, groups), :]))
            right = 0.5 * (c + jnp.where(last_column, 0.0, sigma[l, right_of(e, groups), :]))
            lower = 0.5 * (c + centre[l - 1]) if l > 0 else 0.5 * c
            upper = 0.5 * (c + centre[l + 1]) if l + 1 < layers else 0.5 * c
            diagonal = up + down + left + right + lower + upper + GAMMA * c
            inside = c > 0.0
            inverse = jnp.where(inside, 1.0 / jnp.where(inside, diagonal, 1.0), 0.0)
            coef[0, l, here, :] = up * inverse
            coef[1, l, here, :] = down * inverse
            coef[2, l, here, :] = jnp.where(first_column, 0.0, left * inverse)
            coef[3, l, here, :] = jnp.where(last_column, 0.0, right * inverse)
            if l > 0:
                coef[4, l, here, :] = lower * inverse
            if l + 1 < layers:
                coef[5, l, here, :] = upper * inverse
            if l == 0:
                surface[here, :] = inverse
        return carry

    lax.fori_loop(0, count, body, 0)


def sweep(step, old, new, coef, plane, groups, segments):
    p, g = STEPS[step]
    sources, layers = old.shape[:2]
    count, number = row_numbers(segments)

    def row(e):
        here = dense(e, groups)
        for l in range(layers):
            weight = [coef[i, l, here, :] for i in range(4)]
            lower = coef[4, l, here, :] if l > 0 else None
            upper = coef[5, l, here, :] if l + 1 < layers else None
            for s in range(sources):
                total = p * old[s, l, tile(e, groups), :]
                total += weight[0] * old[s, l, tile(e - 1, groups), :]
                total += weight[1] * old[s, l, tile(e + 1, groups), :]
                total += weight[2] * old[s, l, left_of(e, groups), :]
                total += weight[3] * old[s, l, right_of(e, groups), :]
                if lower is not None:
                    total += lower * old[s, l - 1, tile(e, groups), :]
                if upper is not None:
                    total += upper * old[s, l + 1, tile(e, groups), :]
                if l == 0 and plane is not None:
                    amount = plane[s, here, :]
                    total += amount if g == 1.0 else g * amount
                new[s, l, tile(e, groups), :] = total

    def body(i, carry):
        row(number(2 * i))
        row(number(2 * i + 1))
        return carry

    lax.fori_loop(0, count // 2, body, 0)
    if count % 2:
        row(number(count - 1))


def inner_rows(step, rows):
    return [(HALO + 1 + step, HALO + rows - 1 - step)]


def outer_rows(step, rows):
    return [(1 + step, HALO + 1 + step), (HALO + rows - 1 - step, 2 * HALO + rows - 1 - step)]


def add_electrodes(electrodes_ref, plane, surface, rows, groups, segments):
    columns = groups * LANES
    first_row = lax.axis_index("space") * rows
    lowest, highest = segments[0][0], segments[-1][1] - 1
    column = lax.broadcasted_iota(jnp.int32, (groups, LANES), 1) * groups + lax.broadcasted_iota(
        jnp.int32, (groups, LANES), 0
    )
    for s in range(plane.shape[0]):
        for k, current in enumerate((CURRENT, -CURRENT)):
            node = electrodes_ref[k, s]
            row = node // columns
            e = row - first_row + HALO
            inside = functools.reduce(jnp.logical_or, [(e >= a) & (e < b) for a, b in segments])
            here = dense(jnp.clip(e, lowest, highest), groups)
            hit = (column == node - row * columns) & inside
            plane[s, here, :] += jnp.where(hit, current * surface[here, :], 0.0)


def inner_kernel(groups, electrodes_ref, sigma, _, wide, coef, surface, other, plane):
    rows = extent_of(wide, groups) - 2 * HALO
    segments = inner_rows(0, rows)
    coefficient_rows(sigma, coef, surface, groups, segments)
    plane[...] = jnp.zeros(plane.shape, jnp.float32)
    add_electrodes(electrodes_ref, plane, surface, rows, groups, segments)
    old, new = wide, other
    for step in range(SWEEPS):
        sweep(step, old, new, coef, plane, groups, inner_rows(step, rows))
        refill(planes_of(new), groups, *inner_rows(step, rows)[0])
        old, new = new, old


def inner_solve(groups, electrodes, sigma, wide):
    sources, layers = wide.shape[:2]
    tall = extent_of(wide, groups) * groups
    f32 = jnp.float32
    return pl.pallas_call(
        functools.partial(inner_kernel, groups),
        out_shape=(
            jax.ShapeDtypeStruct(wide.shape, f32),
            jax.ShapeDtypeStruct((6, layers, tall, LANES), f32),
            jax.ShapeDtypeStruct((tall, LANES), f32),
            jax.ShapeDtypeStruct(wide.shape, f32),
            jax.ShapeDtypeStruct((sources, tall, LANES), f32),
        ),
        in_specs=[SMEM, VMEM, VMEM],
        out_specs=(VMEM,) * 5,
        input_output_aliases={2: 0},
        compiler_params=GRANT,
        name="inner",
    )(electrodes, sigma, wide)


def outer_kernel(
    groups, electrodes_ref, sigma_inner, sigma_outer, inner_ref, outer_ref, nodes_ref, *refs
):
    sigma, wide, coef, surface, other, plane, readings_ref = refs[6:]
    sources, layers = wide.shape[:2]
    columns = groups * LANES
    extent = extent_of(wide, groups)
    rows = extent - 2 * HALO
    first_row = lax.axis_index("space") * rows
    from_inner, from_outer = facing("space", rows, False)
    put_rows(sigma, from_inner, sigma_inner, groups)
    put_rows(sigma, from_outer, sigma_outer, groups)
    put_rows(wide, from_inner, inner_ref, groups)
    put_rows(wide, from_outer, outer_ref, groups)
    conductivity = [sigma.at[l] for l in range(layers)]
    for first, last in ((0, HALO), (HALO + rows, extent)):
        refill(conductivity, groups, first, last)
        refill(planes_of(wide), groups, first, last)
    segments = outer_rows(0, rows)
    coefficient_rows(sigma, coef, surface, groups, segments)
    add_electrodes(electrodes_ref, plane, surface, rows, groups, segments)
    old, new = wide, other
    for step in range(SWEEPS):
        sweep(step, old, new, coef, plane, groups, outer_rows(step, rows))
        for first, last in outer_rows(step, rows):
            refill(planes_of(new), groups, first, last)
        old, new = new, old

    node = nodes_ref[...]
    node_row = node // columns
    node_column = node - node_row * columns
    count = node.shape[1]
    picked = jnp.zeros((3 * sources * rows, count), jnp.float32)
    for j in range(groups):
        values = jnp.concatenate([old[s, 0, sublane(HALO, j, rows, groups), :] for s in range(sources)], axis=0)
        picked += jnp.dot(three_parts(values), column_hits(node_column, j, groups), preferred_element_type=jnp.float32)
    size = sources * rows
    picked = picked[:size] + picked[size : 2 * size] + picked[2 * size :]
    r = lax.broadcasted_iota(jnp.int32, (size, count), 0)
    k = lax.broadcasted_iota(jnp.int32, (size, count), 1)
    hit = (r // rows == k // (count // sources)) & (node_row - first_row == r % rows)
    readings_ref[...] = FINAL * jnp.sum(jnp.where(hit, picked, 0.0), axis=0, keepdims=True)


def outer_solve(groups, electrodes, sigma_inner, sigma_outer, from_inner, from_outer, nodes, sigma, inner):
    carried = (sigma,) + tuple(inner)
    f32 = jnp.float32
    kept = tuple(jax.ShapeDtypeStruct(x.shape, f32) for x in carried)
    return pl.pallas_call(
        functools.partial(outer_kernel, groups),
        out_shape=kept + (jax.ShapeDtypeStruct((1, nodes.shape[1]), f32),),
        in_specs=[SMEM] + [VMEM] * 11,
        out_specs=(VMEM,) * 7,
        input_output_aliases={6 + i: i for i in range(6)},
        compiler_params=GRANT,
        name="outer",
    )(electrodes, sigma_inner, sigma_outer, from_inner, from_outer, nodes, *carried)


def begin_kernel(groups, segments, coef, *refs):
    wide, new = refs[-2:]
    extent = extent_of(wide, groups)
    rows = extent - 2 * HALO
    if segments[0][0] == 1:
        from_inner, from_outer = facing("space", rows, False)
        put_rows(wide, from_inner, refs[0], groups)
        put_rows(wide, from_outer, refs[1], groups)
        for first, last in ((0, HALO), (HALO + rows, extent)):
            refill(planes_of(wide), groups, first, last)
    sweep(0, wide, new, coef, None, groups, segments)
    for first, last in segments:
        refill(planes_of(new, range(1, wide.shape[1])), groups, first, last)


def begin_adjoint(groups, segments, coef, halos, wide, new):
    f32 = jnp.float32
    shape = jax.ShapeDtypeStruct(wide.shape, f32)
    halos = halos if segments[0][0] == 1 else ()
    arguments = (coef,) + halos + (wide,) + (() if new is None else (new,))
    at = 1 + len(halos)
    return pl.pallas_call(
        functools.partial(begin_kernel, groups, segments),
        out_shape=(shape, shape),
        in_specs=[VMEM] * len(arguments),
        out_specs=(VMEM, VMEM),
        input_output_aliases={at: 0} if new is None else {at: 0, at + 1: 1},
        compiler_params=GRANT,
        name="begin",
    )(*arguments)


def adjoint_kernel(groups, parts, nodes_ref, observed_ref, coef, surface, forward, *refs):
    readings_refs, refs = refs[:parts], refs[parts + 2 :]
    (wide, new), blocks, (plane, gradient, staged, work) = refs[:2], refs[2:-4], refs[-4:]
    sources, layers = wide.shape[:2]
    columns = groups * LANES
    extent = extent_of(wide, groups)
    rows = extent - 2 * HALO
    count = nodes_ref.shape[1]
    per_source = count // sources
    receivers = per_source // 2
    first_row = lax.axis_index("space") * rows

    lane = lax.broadcasted_iota(jnp.int32, (1, count), 1)
    positive = (lane // receivers) % 2 == 0
    readings = sum(part[...] for part in readings_refs)
    partner = jnp.where(
        positive, pltpu.roll(readings, count - receivers, 1), pltpu.roll(readings, receivers, 1)
    )
    amounts = readings - partner - observed_ref[...]
    node = nodes_ref[...]
    node_row = node // columns
    node_column = node - node_row * columns
    span = extent - 2
    size = sources * span
    r = lax.broadcasted_iota(jnp.int32, (size, count), 0)
    k = lax.broadcasted_iota(jnp.int32, (size, count), 1)
    hit = (r // span == k // per_source) & (node_row - first_row + HALO - 1 == r % span)
    spread = three_parts(jnp.where(hit, amounts, 0.0))
    for j in range(groups):
        part = lax.dot_general(
            spread, column_hits(node_column, j, groups), (((1,), (1,)), ((), ())), preferred_element_type=jnp.float32
        )
        part = part[:size] + part[size : 2 * size] + part[2 * size :]
        where = pl.ds(groups + j, span, stride=groups)
        weight = surface[where, :]
        for s in range(sources):
            amount = part[s * span : (s + 1) * span] * weight
            plane[s, where, :] = amount
            new[s, 0, sublane(1, j, span, groups), :] += amount
    refill(planes_of(new, range(1)), groups, 1, extent - 1)

    old, newer = new, wide
    for step in range(1, SWEEPS):
        segment = (1 + step, extent - 1 - step)
        sweep(step, old, newer, coef, plane, groups, [segment])
        refill(planes_of(newer), groups, *segment)
        old, newer = newer, old
    adjoint = old

    first_column, last_column = end_masks(groups)
    first_sublane = lax.broadcasted_iota(jnp.int32, (groups, LANES), 0) == 0

    def row(e, above_faces):
        here, below, right_here = tile(e, groups), tile(e + 1, groups), right_of(e, groups)
        sums = []
        for l in range(layers):
            for s in range(sources):
                u, a = forward[s, l, here, :], adjoint[s, l, here, :]
                terms = [
                    u * a,
                    (u - forward[s, l, below, :]) * (a - adjoint[s, l, below, :]),
                    (u - forward[s, l, right_here, :]) * (a - adjoint[s, l, right_here, :]),
                ]
                if l + 1 < layers:
                    terms.append((u - forward[s, l + 1, here, :]) * (a - adjoint[s, l + 1, here, :]))
                total = terms if s == 0 else [x + y for x, y in zip(total, terms)]
            sums.append(total)
        for l in range(layers):
            product, down, right = sums[l][:3]
            right = jnp.where(last_column, product, right)
            turned = pltpu.roll(right, 1, 0)
            left = jnp.where(first_sublane, pltpu.roll(turned, 1, 1), turned)
            left = jnp.where(first_column, product, left)
            upper = sums[l][3] if l + 1 < layers else product
            lower = sums[l - 1][3] if l > 0 else product
            total = product + above_faces[l] + down + right + left + lower + upper
            gradient[l, dense(e - HALO, groups), :] = (-0.5 * FINAL * FINAL) * total
        return tuple(sums[l][1] for l in range(layers))

    above_faces = []
    for l in range(layers):
        for s in range(sources):
            above, here = tile(HALO - 1, groups), tile(HALO, groups)
            term = (forward[s, l, above, :] - forward[s, l, here, :]) * (
                adjoint[s, l, above, :] - adjoint[s, l, here, :]
            )
            total = term if s == 0 else total + term
        above_faces.append(total)

    lax.fori_loop(HALO, HALO + rows, row, tuple(above_faces))

    count_blocks = len(blocks)
    me = lax.axis_index("src") if count_blocks > 1 else 0
    per = groups // count_blocks

    def read(j):
        return jnp.concatenate([gradient[l, pl.ds(j, rows, stride=groups), :] for l in range(layers)], axis=0)

    def write(j, turned):
        for l in range(layers):
            staged[j // per, l, :, (j % per) * LANES : (j % per + 1) * LANES] = turned[l * rows : (l + 1) * rows]

    columns_to_lanes(read, write, work, groups)
    for i, block in enumerate(blocks):
        block[...] = staged[me ^ i]


def finish_adjoint(groups, nodes, readings, observed, wide, new, coef, surface, forward, blocks):
    sources, layers = wide.shape[:2]
    extent = extent_of(wide, groups)
    tall = extent * groups
    rows = extent - 2 * HALO
    columns = groups * LANES
    f32 = jnp.float32
    block = jax.ShapeDtypeStruct((layers, rows, columns // blocks), f32)
    shape = jax.ShapeDtypeStruct(wide.shape, f32)
    parts = len(readings)
    return pl.pallas_call(
        functools.partial(adjoint_kernel, groups, parts),
        out_shape=(shape, shape) + (block,) * blocks,
        in_specs=[VMEM] * (7 + parts),
        out_specs=(VMEM,) * (2 + blocks),
        scratch_shapes=[
            pltpu.VMEM((sources, tall, LANES), f32),
            pltpu.VMEM((layers, rows * groups, LANES), f32),
            pltpu.VMEM((blocks, layers, rows, columns // blocks), f32),
            pltpu.VMEM((columns, LANES), f32),
        ],
        input_output_aliases={5 + parts: 0, 6 + parts: 1},
        compiler_params=GRANT,
        name="adjoint",
    )(nodes, observed, coef, surface, forward, *readings, wide, new)[2:]


def is_power_of_two(n):
    return n & (n - 1) == 0


def exchange(value, axis, mask):
    count = lax.axis_size(axis)
    return lax.ppermute(value, axis, [(i, i ^ mask) for i in range(count)])


def neighbour_pairs(value, axis, first):
    lower = range(first, lax.axis_size(axis) - 1, 2)
    return lax.ppermute(value, axis, [(i, i + 1) for i in lower] + [(i + 1, i) for i in lower])


def per_device(potential_start, adjoint_start, conductivity, electrodes, receivers, observed):
    _, _, rows, columns = potential_start.shape
    groups = columns // LANES
    split, strips = lax.axis_size("src"), lax.axis_size("space")
    direct = is_power_of_two(split) and split <= 4 and (columns // split) % LANES == 0

    if direct:
        pieces = [conductivity] + [None] * (split - 1)
        for k in reversed(range(1, split)):
            pieces[k] = exchange(conductivity, "src", k)
    else:
        pieces = [lax.all_gather(conductivity, "src", axis=2, tiled=True)]
    x_wide, to_inner, to_outer = spread_rows(potential_start)
    from_inner = neighbour_pairs(to_inner, "space", 0)
    from_outer = neighbour_pairs(to_outer, "space", 1)
    a_wide, a_inner, a_outer = spread_rows(adjoint_start)
    a_inner = neighbour_pairs(a_inner, "space", 0)
    a_outer = neighbour_pairs(a_outer, "space", 1)
    nodes, measured = lay_out_nodes(receivers.transpose(0, 2, 1), observed)
    sigma, sigma_inner, sigma_outer = assemble_sigma(pieces, groups)
    sigma_outer = neighbour_pairs(sigma_outer, "space", 1)
    sigma_inner = neighbour_pairs(sigma_inner, "space", 0)
    ends = electrodes.T
    inner = inner_solve(groups, ends, sigma, x_wide)
    _, forward, coef, surface, _, _, readings = outer_solve(
        groups, ends, sigma_inner, sigma_outer, from_inner, from_outer, nodes, sigma, inner
    )

    parts, begun = [inner_rows(0, rows), outer_rows(0, rows)], None

    def begin(wide, new):
        return begin_adjoint(groups, parts.pop(0), coef, (a_inner, a_outer), wide, new)

    if is_power_of_two(strips):
        rounds = strips.bit_length() - 1
        for i in range(rounds):
            other = exchange(readings, "space", 1 << i)
            if i >= rounds - 2:
                a_wide, begun = begin(a_wide, begun)
            if i + 1 < rounds:
                readings = readings + other
        terms = [readings, other] if rounds else [readings]
    else:
        terms = [lax.psum(readings, "space")]
    while parts:
        a_wide, begun = begin(a_wide, begun)
    blocks = finish_adjoint(
        groups, nodes, terms, measured, a_wide, begun, coef, surface, forward, split if direct else 1
    )
    if direct:
        total = blocks[0]
        for k in reversed(range(1, split)):
            total = total + exchange(blocks[k], "src", k)
        return total
    summed = lax.psum(blocks[0], "src")
    share = columns // split
    return lax.dynamic_slice_in_dim(summed, lax.axis_index("src") * share, share, 2)


def solution(mesh):
    return jax.shard_map(
        per_device,
        mesh=mesh,
        in_specs=(
            P("src", None, "space", None),
            P("src", None, "space", None),
            P(None, "space", "src"),
            P("src", None),
            P("src", None, None),
            P("src", None),
        ),
        out_specs=P(None, "space", "src"),
        check_vma=False,
    )
```

```python
import functools
import math

import jax
import jax.numpy as jnp
from jax import lax
from jax.experimental import pallas as pl
from jax.experimental.pallas import tpu as pltpu
from jax.sharding import PartitionSpec as P


SWEEPS = 4
GAMMA = 0.5
CURRENT = 4.0
THETA = 1.025
DELTA = 0.975
LANES = 128
HALO = SWEEPS + 1
BATCH = 8

VMEM = pl.BlockSpec(memory_space=pltpu.VMEM)
SMEM = pl.BlockSpec(memory_space=pltpu.SMEM)
GRANT = pltpu.CompilerParams(vmem_limit_bytes=20 * 1024 * 1024)


def product_form():
    roots = [THETA + DELTA * math.cos((2 * i + 1) * math.pi / (2 * SWEEPS)) for i in range(SWEEPS)]
    order = sorted(roots)
    order = [order[i // 2] if i % 2 == 0 else order[-1 - i // 2] for i in range(SWEEPS)]
    steps, scale = [], 1.0
    for root in order:
        steps.append((root - 1.0, 1.0 / scale))
        scale /= root
    return steps, scale


STEPS, FINAL = product_form()


def dense(e, groups):
    begin = e * groups
    return pl.ds(begin if isinstance(begin, int) else pl.multiple_of(begin, groups), groups)


def tile(e, groups):
    begin = (2 * e + 1) * groups
    return pl.ds(begin if isinstance(begin, int) else pl.multiple_of(begin, groups), groups)


def left_of(e, groups):
    return pl.ds((2 * e + 1) * groups - 1, groups)


def right_of(e, groups):
    return pl.ds((2 * e + 1) * groups + 1, groups)


def sublane(first, j, count, groups):
    return pl.ds((2 * first + 1) * groups + j, count, stride=2 * groups)


def extent_of(wide, groups):
    return wide.shape[-2] // (2 * groups) - 1


def wide_length(rows, columns):
    return (rows + 2 * HALO + 1) * 2 * (columns // LANES)


def refill(planes, groups, start):
    for plane in planes:
        plane[sublane(start, -1, BATCH, groups), :] = pltpu.roll(plane[sublane(start, groups - 1, BATCH, groups), :], 1, 1)
        plane[sublane(start, groups, BATCH, groups), :] = pltpu.roll(
            plane[sublane(start, 0, BATCH, groups), :], LANES - 1, 1
        )


def refill_rows(planes, groups, first, last):
    for start in range(first, last, BATCH):
        refill(planes, groups, min(start, extent_of(planes[0], groups) - BATCH))


def refill_two(planes, groups, low, high):
    def both(plane, j):
        return jnp.concatenate([plane[sublane(at, j, SWEEPS, groups), :] for at in (low, high)], axis=0)

    for plane in planes:
        left = pltpu.roll(both(plane, groups - 1), 1, 1)
        right = pltpu.roll(both(plane, 0), LANES - 1, 1)
        for i, at in enumerate((low, high)):
            plane[sublane(at, -1, SWEEPS, groups), :] = left[i * SWEEPS : (i + 1) * SWEEPS]
            plane[sublane(at, groups, SWEEPS, groups), :] = right[i * SWEEPS : (i + 1) * SWEEPS]


def planes_of(field, layers=None):
    layers = range(field.shape[1]) if layers is None else layers
    return [field.at[s, l] for s in range(field.shape[0]) for l in layers]


def doubled(rows):
    count = rows.shape[0]
    if count == LANES:
        return rows
    return jnp.concatenate([rows] * (LANES // count) + ([rows[: LANES % count]] if LANES % count else []), axis=0)


def columns_to_sublanes(read, write, work, groups):
    for j in range(groups):
        work[j * LANES : (j + 1) * LANES, :] = doubled(read(j)).T
    for s in range(groups):
        write(s, work[pl.ds(s, LANES, stride=groups), :].T)


def columns_to_lanes(read, write, work, groups):
    for s in range(groups):
        work[pl.ds(s, LANES, stride=groups), :] = doubled(read(s)).T
    for j in range(groups):
        write(j, work[j * LANES : (j + 1) * LANES, :].T)


def end_masks(groups):
    lane = lax.broadcasted_iota(jnp.int32, (groups, LANES), 1)
    group = lax.broadcasted_iota(jnp.int32, (groups, LANES), 0)
    return (lane == 0) & (group == 0), (lane == LANES - 1) & (group == groups - 1)


def three_parts(x):
    high = x.astype(jnp.bfloat16)
    rest = x - high.astype(jnp.float32)
    middle = rest.astype(jnp.bfloat16)
    low = (rest - middle.astype(jnp.float32)).astype(jnp.bfloat16)
    return jnp.concatenate([high, middle, low], axis=0)


def column_hits(columns, j, groups):
    nodes = columns.shape[1]
    c = lax.broadcasted_iota(jnp.int32, (LANES, nodes), 0) * groups + j
    return jnp.where(c == columns, 1.0, 0.0).astype(jnp.bfloat16)


def facing(axis, rows, sent):
    even = lax.rem(lax.axis_index(axis), 2) == 0
    low, high = (HALO, rows) if sent else (0, HALO + rows)
    return jnp.where(even, high, low), jnp.where(even, low, high)


def take_rows(wide, first, out, groups):
    for h in range(HALO):
        out[..., h * groups : (h + 1) * groups, :] = wide[..., tile(first + h, groups), :]


def put_rows(wide, first, received, groups):
    for h in range(HALO):
        wide[..., tile(first + h, groups), :] = received[..., h * groups : (h + 1) * groups, :]


def spread_kernel(groups, complete, x_ref, wide, inner_ref, outer_ref, work):
    sources, layers, rows, _ = x_ref.shape
    fields = [(s, l) for s in range(sources) for l in range(layers)]
    per = LANES // rows
    for at in range(0, len(fields), per):
        block = fields[at : at + per]

        def read(j):
            return jnp.concatenate([x_ref[s, l, :, j * LANES : (j + 1) * LANES] for s, l in block], axis=0)

        def write(j, turned):
            for i, (s, l) in enumerate(block):
                wide[s, l, sublane(HALO, j, rows, groups), :] = turned[i * rows : (i + 1) * rows]

        columns_to_sublanes(read, write, work, groups)
    if complete:
        refill_rows(planes_of(wide), groups, HALO, HALO + rows)
    to_inner, to_outer = facing("space", rows, True)
    take_rows(wide, to_inner, inner_ref, groups)
    take_rows(wide, to_outer, outer_ref, groups)


def spread_rows(x, complete):
    sources, layers, rows, columns = x.shape
    groups = columns // LANES
    wide = jax.ShapeDtypeStruct((sources, layers, wide_length(rows, columns), LANES), jnp.float32)
    halo = jax.ShapeDtypeStruct((sources, layers, HALO * groups, LANES), jnp.float32)
    return pl.pallas_call(
        functools.partial(spread_kernel, groups, complete),
        out_shape=(wide, halo, halo),
        in_specs=[VMEM],
        out_specs=(VMEM,) * 3,
        scratch_shapes=[pltpu.VMEM((columns, LANES), jnp.float32)],
        compiler_params=GRANT,
        name="spread",
    )(x)


def nodes_kernel(receivers_ref, observed_ref, nodes_ref, measured_ref):
    sources, ends, count = receivers_ref.shape
    for s in range(sources):
        for end in range(ends):
            lanes = pl.ds((s * ends + end) * count, count)
            nodes_ref[:, lanes] = receivers_ref[s, end : end + 1, :]
            seen = observed_ref[s : s + 1, :]
            measured_ref[:, lanes] = seen if end == 0 else -seen


def lay_out_nodes(receivers, observed):
    sources, ends, count = receivers.shape
    total = sources * ends * count
    return pl.pallas_call(
        nodes_kernel,
        out_shape=(
            jax.ShapeDtypeStruct((1, total), jnp.int32),
            jax.ShapeDtypeStruct((1, total), jnp.float32),
        ),
        in_specs=[VMEM] * 2,
        out_specs=(VMEM,) * 2,
        compiler_params=GRANT,
        name="nodes",
    )(receivers, observed)


def sigma_kernel(groups, *refs):
    pieces, (wide_ref, inner_ref, outer_ref, stage, work) = refs[:-5], refs[-5:]
    count = len(pieces)
    layers, rows, share = pieces[0].shape
    me = lax.axis_index("src") if count > 1 else 0
    for k, piece in enumerate(pieces):
        stage[me ^ k] = piece[...]
    per = share // LANES

    def read(j):
        return stage[j // per, :, :, (j % per) * LANES : (j % per + 1) * LANES].reshape(layers * rows, LANES)

    def write(j, turned):
        for l in range(layers):
            wide_ref[l, sublane(HALO, j, rows, groups), :] = turned[l * rows : (l + 1) * rows]

    columns_to_sublanes(read, write, work, groups)
    refill_rows([wide_ref.at[l] for l in range(layers)], groups, HALO, HALO + rows)
    to_inner, to_outer = facing("space", rows, True)
    take_rows(wide_ref, to_inner, inner_ref, groups)
    take_rows(wide_ref, to_outer, outer_ref, groups)


def assemble_sigma(pieces, groups):
    layers, rows, share = pieces[0].shape
    columns = groups * LANES
    wide = jax.ShapeDtypeStruct((layers, wide_length(rows, columns), LANES), jnp.float32)
    halo = jax.ShapeDtypeStruct((layers, HALO * groups, LANES), jnp.float32)
    return pl.pallas_call(
        functools.partial(sigma_kernel, groups),
        out_shape=(wide, halo, halo),
        in_specs=[VMEM] * len(pieces),
        out_specs=(VMEM, VMEM, VMEM),
        scratch_shapes=[
            pltpu.VMEM((len(pieces), layers, rows, share), jnp.float32),
            pltpu.VMEM((columns, LANES), jnp.float32),
        ],
        compiler_params=GRANT,
        name="sigma",
    )(*pieces)


def row_numbers(segments):
    (first, middle), count = segments[0], segments[0][1] - segments[0][0]
    if len(segments) == 1:
        return count, lambda i: first + i
    start, end = segments[1]

    def number(i):
        if isinstance(i, int):
            return first + i if i < count else start + i - count
        return first + i + jnp.where(i >= count, start - middle, 0)

    return count + end - start, number


def coefficient_rows(sigma, coef, surface, groups, segments):
    layers = sigma.shape[0]
    first_column, last_column = end_masks(groups)
    count, number = row_numbers(segments)

    def body(i, carry):
        e = number(i)
        here = dense(e, groups)
        centre = [sigma[l, tile(e, groups), :] for l in range(layers)]
        for l in range(layers):
            c = centre[l]
            up = 0.5 * (c + sigma[l, tile(e - 1, groups), :])
            down = 0.5 * (c + sigma[l, tile(e + 1, groups), :])
            left = 0.5 * (c + jnp.where(first_column, 0.0, sigma[l, left_of(e, groups), :]))
            right = 0.5 * (c + jnp.where(last_column, 0.0, sigma[l, right_of(e, groups), :]))
            lower = 0.5 * (c + centre[l - 1]) if l > 0 else 0.5 * c
            upper = 0.5 * (c + centre[l + 1]) if l + 1 < layers else 0.5 * c
            diagonal = up + down + left + right + lower + upper + GAMMA * c
            inside = c > 0.0
            inverse = jnp.where(inside, 1.0 / jnp.where(inside, diagonal, 1.0), 0.0)
            coef[0, l, here, :] = up * inverse
            coef[1, l, here, :] = down * inverse
            coef[2, l, here, :] = jnp.where(first_column, 0.0, left * inverse)
            coef[3, l, here, :] = jnp.where(last_column, 0.0, right * inverse)
            if l > 0:
                coef[4, l, here, :] = lower * inverse
            if l + 1 < layers:
                coef[5, l, here, :] = upper * inverse
            if l == 0:
                surface[here, :] = inverse
        return carry

    lax.fori_loop(0, count, body, 0)


def sweep(step, old, new, coef, plane, groups, segments, layers_refilled=None):
    p, g = STEPS[step]
    sources, layers = old.shape[:2]
    count, number = row_numbers(segments)

    def row(e):
        here = dense(e, groups)
        for l in range(layers):
            weight = [coef[i, l, here, :] for i in range(4)]
            lower = coef[4, l, here, :] if l > 0 else None
            upper = coef[5, l, here, :] if l + 1 < layers else None
            for s in range(sources):
                total = p * old[s, l, tile(e, groups), :]
                total += weight[0] * old[s, l, tile(e - 1, groups), :]
                total += weight[1] * old[s, l, tile(e + 1, groups), :]
                total += weight[2] * old[s, l, left_of(e, groups), :]
                total += weight[3] * old[s, l, right_of(e, groups), :]
                if lower is not None:
                    total += lower * old[s, l - 1, tile(e, groups), :]
                if upper is not None:
                    total += upper * old[s, l + 1, tile(e, groups), :]
                if l == 0 and plane is not None:
                    amount = plane[s, here, :]
                    total += amount if g == 1.0 else g * amount
                new[s, l, tile(e, groups), :] = total

    if len(segments) > 1:

        def body(i, carry):
            row(number(2 * i))
            row(number(2 * i + 1))
            return carry

        lax.fori_loop(0, count // 2, body, 0)
        if count % 2:
            row(number(count - 1))
        return

    first, last = segments[0]
    planes = planes_of(new, layers_refilled)

    edge = extent_of(new, groups) - BATCH
    for start in range(first, last, BATCH):
        for e in range(start, min(start + BATCH, last)):
            row(e)
        refill(planes, groups, min(start, edge))


def inner_rows(step, rows):
    return [(HALO + 1 + step, HALO + rows - 1 - step)]


def outer_rows(step, rows):
    return [(1 + step, HALO + 1 + step), (HALO + rows - 1 - step, 2 * HALO + rows - 1 - step)]


def add_electrodes(electrodes_ref, plane, surface, rows, groups, segments):
    columns = groups * LANES
    first_row = lax.axis_index("space") * rows
    lowest, highest = segments[0][0], segments[-1][1] - 1
    column = lax.broadcasted_iota(jnp.int32, (groups, LANES), 1) * groups + lax.broadcasted_iota(
        jnp.int32, (groups, LANES), 0
    )
    for s in range(plane.shape[0]):
        for k, current in enumerate((CURRENT, -CURRENT)):
            node = electrodes_ref[k, s]
            row = node // columns
            e = row - first_row + HALO
            inside = functools.reduce(jnp.logical_or, [(e >= a) & (e < b) for a, b in segments])
            here = dense(jnp.clip(e, lowest, highest), groups)
            hit = (column == node - row * columns) & inside
            plane[s, here, :] += jnp.where(hit, current * surface[here, :], 0.0)


def inner_kernel(groups, electrodes_ref, sigma, _, wide, coef, surface, other, plane):
    rows = extent_of(wide, groups) - 2 * HALO
    segments = inner_rows(0, rows)
    coefficient_rows(sigma, coef, surface, groups, segments)
    plane[...] = jnp.zeros(plane.shape, jnp.float32)
    add_electrodes(electrodes_ref, plane, surface, rows, groups, segments)
    old, new = wide, other
    for step in range(SWEEPS):
        sweep(step, old, new, coef, plane, groups, inner_rows(step, rows))
        old, new = new, old


def inner_solve(groups, electrodes, sigma, wide):
    sources, layers = wide.shape[:2]
    tall = extent_of(wide, groups) * groups
    f32 = jnp.float32
    return pl.pallas_call(
        functools.partial(inner_kernel, groups),
        out_shape=(
            jax.ShapeDtypeStruct(wide.shape, f32),
            jax.ShapeDtypeStruct((6, layers, tall, LANES), f32),
            jax.ShapeDtypeStruct((tall, LANES), f32),
            jax.ShapeDtypeStruct(wide.shape, f32),
            jax.ShapeDtypeStruct((sources, tall, LANES), f32),
        ),
        in_specs=[SMEM, VMEM, VMEM],
        out_specs=(VMEM,) * 5,
        input_output_aliases={2: 0},
        compiler_params=GRANT,
        name="inner",
    )(electrodes, sigma, wide)


def outer_kernel(
    groups, electrodes_ref, sigma_inner, sigma_outer, inner_ref, outer_ref, nodes_ref, *refs
):
    sigma, wide, coef, surface, other, plane, readings_ref = refs[6:]
    sources, layers = wide.shape[:2]
    columns = groups * LANES
    extent = extent_of(wide, groups)
    rows = extent - 2 * HALO
    first_row = lax.axis_index("space") * rows
    from_inner, from_outer = facing("space", rows, False)
    put_rows(sigma, from_inner, sigma_inner, groups)
    put_rows(sigma, from_outer, sigma_outer, groups)
    put_rows(wide, from_inner, inner_ref, groups)
    put_rows(wide, from_outer, outer_ref, groups)
    refill_two([sigma.at[l] for l in range(layers)], groups, 1, extent - 1 - SWEEPS)
    refill_two(planes_of(wide), groups, 1, extent - 1 - SWEEPS)
    segments = outer_rows(0, rows)
    coefficient_rows(sigma, coef, surface, groups, segments)
    add_electrodes(electrodes_ref, plane, surface, rows, groups, segments)
    old, new = wide, other
    for step in range(SWEEPS):
        sweep(step, old, new, coef, plane, groups, outer_rows(step, rows))
        (first, _), (_, last) = outer_rows(step, rows)
        refill_two(planes_of(new), groups, first + 1, last - 1 - SWEEPS)
        old, new = new, old

    node = nodes_ref[...]
    node_row = node // columns
    node_column = node - node_row * columns
    count = node.shape[1]
    picked = jnp.zeros((3 * sources * rows, count), jnp.float32)
    for j in range(groups):
        values = jnp.concatenate([old[s, 0, sublane(HALO, j, rows, groups), :] for s in range(sources)], axis=0)
        picked += jnp.dot(three_parts(values), column_hits(node_column, j, groups), preferred_element_type=jnp.float32)
    size = sources * rows
    picked = picked[:size] + picked[size : 2 * size] + picked[2 * size :]
    r = lax.broadcasted_iota(jnp.int32, (size, count), 0)
    k = lax.broadcasted_iota(jnp.int32, (size, count), 1)
    hit = (r // rows == k // (count // sources)) & (node_row - first_row == r % rows)
    readings_ref[...] = FINAL * jnp.sum(jnp.where(hit, picked, 0.0), axis=0, keepdims=True)


def outer_solve(groups, electrodes, sigma_inner, sigma_outer, from_inner, from_outer, nodes, sigma, inner):
    carried = (sigma,) + tuple(inner)
    f32 = jnp.float32
    kept = tuple(jax.ShapeDtypeStruct(x.shape, f32) for x in carried)
    return pl.pallas_call(
        functools.partial(outer_kernel, groups),
        out_shape=kept + (jax.ShapeDtypeStruct((1, nodes.shape[1]), f32),),
        in_specs=[SMEM] + [VMEM] * 11,
        out_specs=(VMEM,) * 7,
        input_output_aliases={6 + i: i for i in range(6)},
        compiler_params=GRANT,
        name="outer",
    )(electrodes, sigma_inner, sigma_outer, from_inner, from_outer, nodes, *carried)


def begin_kernel(groups, segments, coef, *refs):
    wide, new = refs[-2:]
    extent = extent_of(wide, groups)
    rows = extent - 2 * HALO
    if segments[0][0] == 1:
        from_inner, from_outer = facing("space", rows, False)
        put_rows(wide, from_inner, refs[0], groups)
        put_rows(wide, from_outer, refs[1], groups)
        refill_two(planes_of(wide), groups, 1, extent - 1 - SWEEPS)
    else:
        refill_rows(planes_of(wide), groups, HALO, HALO + rows)
    above_surface = range(1, wide.shape[1])
    sweep(0, wide, new, coef, None, groups, segments, above_surface)
    if len(segments) > 1:
        refill_two(planes_of(new, above_surface), groups, segments[0][0] + 1, segments[1][1] - 1 - SWEEPS)


def begin_adjoint(groups, segments, coef, halos, wide, new):
    f32 = jnp.float32
    shape = jax.ShapeDtypeStruct(wide.shape, f32)
    halos = halos if segments[0][0] == 1 else ()
    arguments = (coef,) + halos + (wide,) + (() if new is None else (new,))
    at = 1 + len(halos)
    return pl.pallas_call(
        functools.partial(begin_kernel, groups, segments),
        out_shape=(shape, shape),
        in_specs=[VMEM] * len(arguments),
        out_specs=(VMEM, VMEM),
        input_output_aliases={at: 0} if new is None else {at: 0, at + 1: 1},
        compiler_params=GRANT,
        name="begin",
    )(*arguments)


def adjoint_kernel(groups, parts, nodes_ref, observed_ref, coef, surface, forward, *refs):
    readings_refs, refs = refs[:parts], refs[parts + 2 :]
    (wide, new), blocks, (plane, gradient, staged, work) = refs[:2], refs[2:-4], refs[-4:]
    sources, layers = wide.shape[:2]
    columns = groups * LANES
    extent = extent_of(wide, groups)
    rows = extent - 2 * HALO
    count = nodes_ref.shape[1]
    per_source = count // sources
    receivers = per_source // 2
    first_row = lax.axis_index("space") * rows

    lane = lax.broadcasted_iota(jnp.int32, (1, count), 1)
    positive = (lane // receivers) % 2 == 0
    readings = sum(part[...] for part in readings_refs)
    partner = jnp.where(
        positive, pltpu.roll(readings, count - receivers, 1), pltpu.roll(readings, receivers, 1)
    )
    amounts = readings - partner - observed_ref[...]
    node = nodes_ref[...]
    node_row = node // columns
    node_column = node - node_row * columns
    span = extent - 2
    size = sources * span
    r = lax.broadcasted_iota(jnp.int32, (size, count), 0)
    k = lax.broadcasted_iota(jnp.int32, (size, count), 1)
    hit = (r // span == k // per_source) & (node_row - first_row + HALO - 1 == r % span)
    spread = three_parts(jnp.where(hit, amounts, 0.0))
    for j in range(groups):
        part = lax.dot_general(
            spread, column_hits(node_column, j, groups), (((1,), (1,)), ((), ())), preferred_element_type=jnp.float32
        )
        part = part[:size] + part[size : 2 * size] + part[2 * size :]
        where = pl.ds(groups + j, span, stride=groups)
        weight = surface[where, :]
        for s in range(sources):
            amount = part[s * span : (s + 1) * span] * weight
            plane[s, where, :] = amount
            new[s, 0, sublane(1, j, span, groups), :] += amount
    refill_rows(planes_of(new, range(1)), groups, 1, extent - 1)

    old, newer = new, wide
    for step in range(1, SWEEPS):
        segment = (1 + step, extent - 1 - step)
        sweep(step, old, newer, coef, plane, groups, [segment])
        old, newer = newer, old
    adjoint = old

    first_column, last_column = end_masks(groups)
    first_sublane = lax.broadcasted_iota(jnp.int32, (groups, LANES), 0) == 0

    def row(e, above_faces):
        here, below, right_here = tile(e, groups), tile(e + 1, groups), right_of(e, groups)
        sums = []
        for l in range(layers):
            for s in range(sources):
                u, a = forward[s, l, here, :], adjoint[s, l, here, :]
                terms = [
                    u * a,
                    (u - forward[s, l, below, :]) * (a - adjoint[s, l, below, :]),
                    (u - forward[s, l, right_here, :]) * (a - adjoint[s, l, right_here, :]),
                ]
                if l + 1 < layers:
                    terms.append((u - forward[s, l + 1, here, :]) * (a - adjoint[s, l + 1, here, :]))
                total = terms if s == 0 else [x + y for x, y in zip(total, terms)]
            sums.append(total)
        for l in range(layers):
            product, down, right = sums[l][:3]
            right = jnp.where(last_column, product, right)
            turned = pltpu.roll(right, 1, 0)
            left = jnp.where(first_sublane, pltpu.roll(turned, 1, 1), turned)
            left = jnp.where(first_column, product, left)
            upper = sums[l][3] if l + 1 < layers else product
            lower = sums[l - 1][3] if l > 0 else product
            total = product + above_faces[l] + down + right + left + lower + upper
            gradient[l, dense(e - HALO, groups), :] = (-0.5 * FINAL * FINAL) * total
        return tuple(sums[l][1] for l in range(layers))

    above_faces = []
    for l in range(layers):
        for s in range(sources):
            above, here = tile(HALO - 1, groups), tile(HALO, groups)
            term = (forward[s, l, above, :] - forward[s, l, here, :]) * (
                adjoint[s, l, above, :] - adjoint[s, l, here, :]
            )
            total = term if s == 0 else total + term
        above_faces.append(total)

    def two_rows(i, above_faces):
        return row(HALO + 2 * i + 1, row(HALO + 2 * i, above_faces))

    above_faces = lax.fori_loop(0, rows // 2, two_rows, tuple(above_faces))
    if rows % 2:
        row(HALO + rows - 1, above_faces)

    count_blocks = len(blocks)
    me = lax.axis_index("src") if count_blocks > 1 else 0
    per = groups // count_blocks

    def read(j):
        return jnp.concatenate([gradient[l, pl.ds(j, rows, stride=groups), :] for l in range(layers)], axis=0)

    def write(j, turned):
        for l in range(layers):
            staged[j // per, l, :, (j % per) * LANES : (j % per + 1) * LANES] = turned[l * rows : (l + 1) * rows]

    columns_to_lanes(read, write, work, groups)
    for i, block in enumerate(blocks):
        block[...] = staged[me ^ i]


def finish_adjoint(groups, nodes, readings, observed, wide, new, coef, surface, forward, blocks):
    sources, layers = wide.shape[:2]
    extent = extent_of(wide, groups)
    tall = extent * groups
    rows = extent - 2 * HALO
    columns = groups * LANES
    f32 = jnp.float32
    block = jax.ShapeDtypeStruct((layers, rows, columns // blocks), f32)
    shape = jax.ShapeDtypeStruct(wide.shape, f32)
    parts = len(readings)
    return pl.pallas_call(
        functools.partial(adjoint_kernel, groups, parts),
        out_shape=(shape, shape) + (block,) * blocks,
        in_specs=[VMEM] * (7 + parts),
        out_specs=(VMEM,) * (2 + blocks),
        scratch_shapes=[
            pltpu.VMEM((sources, tall, LANES), f32),
            pltpu.VMEM((layers, rows * groups, LANES), f32),
            pltpu.VMEM((blocks, layers, rows, columns // blocks), f32),
            pltpu.VMEM((columns, LANES), f32),
        ],
        input_output_aliases={5 + parts: 0, 6 + parts: 1},
        compiler_params=GRANT,
        name="adjoint",
    )(nodes, observed, coef, surface, forward, *readings, wide, new)[2:]


def is_power_of_two(n):
    return n & (n - 1) == 0


def exchange(value, axis, mask):
    count = lax.axis_size(axis)
    return lax.ppermute(value, axis, [(i, i ^ mask) for i in range(count)])


def neighbour_pairs(value, axis, first):
    lower = range(first, lax.axis_size(axis) - 1, 2)
    return lax.ppermute(value, axis, [(i, i + 1) for i in lower] + [(i + 1, i) for i in lower])


def per_device(potential_start, adjoint_start, conductivity, electrodes, receivers, observed):
    _, _, rows, columns = potential_start.shape
    groups = columns // LANES
    split, strips = lax.axis_size("src"), lax.axis_size("space")
    direct = is_power_of_two(split) and split <= 4 and (columns // split) % LANES == 0

    if direct:
        pieces = [conductivity] + [None] * (split - 1)
        for k in reversed(range(1, split)):
            pieces[k] = exchange(conductivity, "src", k)
    else:
        pieces = [lax.all_gather(conductivity, "src", axis=2, tiled=True)]
    x_wide, to_inner, to_outer = spread_rows(potential_start, True)
    from_inner = neighbour_pairs(to_inner, "space", 0)
    from_outer = neighbour_pairs(to_outer, "space", 1)
    a_wide, a_inner, a_outer = spread_rows(adjoint_start, False)
    a_inner = neighbour_pairs(a_inner, "space", 0)
    a_outer = neighbour_pairs(a_outer, "space", 1)
    nodes, measured = lay_out_nodes(receivers.transpose(0, 2, 1), observed)
    ends = electrodes.T
    sigma, sigma_inner, sigma_outer = assemble_sigma(pieces, groups)
    sigma_outer = neighbour_pairs(sigma_outer, "space", 1)
    sigma_inner = neighbour_pairs(sigma_inner, "space", 0)
    inner = inner_solve(groups, ends, sigma, x_wide)
    _, forward, coef, surface, _, _, readings = outer_solve(
        groups, ends, sigma_inner, sigma_outer, from_inner, from_outer, nodes, sigma, inner
    )

    parts, begun = [inner_rows(0, rows), outer_rows(0, rows)], None

    def begin(wide, new):
        return begin_adjoint(groups, parts.pop(0), coef, (a_inner, a_outer), wide, new)

    if is_power_of_two(strips):
        rounds = strips.bit_length() - 1
        for i in range(rounds):
            other = exchange(readings, "space", 1 << i)
            if i >= rounds - 2:
                a_wide, begun = begin(a_wide, begun)
            if i + 1 < rounds:
                readings = readings + other
        terms = [readings, other] if rounds else [readings]
    else:
        terms = [lax.psum(readings, "space")]
    while parts:
        a_wide, begun = begin(a_wide, begun)
    blocks = finish_adjoint(
        groups, nodes, terms, measured, a_wide, begun, coef, surface, forward, split if direct else 1
    )
    if direct:
        total = blocks[0]
        for k in reversed(range(1, split)):
            total = total + exchange(blocks[k], "src", k)
        return total
    summed = lax.psum(blocks[0], "src")
    share = columns // split
    return lax.dynamic_slice_in_dim(summed, lax.axis_index("src") * share, share, 2)


def solution(mesh):
    return jax.shard_map(
        per_device,
        mesh=mesh,
        in_specs=(
            P("src", None, "space", None),
            P("src", None, "space", None),
            P(None, "space", "src"),
            P("src", None),
            P("src", None, None),
            P("src", None),
        ),
        out_specs=P(None, "space", "src"),
        check_vma=False,
    )
```
